32 devices in a mesh: outer: 8 (over y, x, core), inner: 4 (over z).
Axes of the slice: x: 2, y: 2, z: 4, core: 2. Of those that a mesh axis runs over, the one named last changes fastest.
Arguments:
- query_image: bfloat16 [2048, 1024], P(('outer', 'inner')), may hold values from -6 to 6
- key_image: bfloat16 [2048, 1024], P(('outer', 'inner')), may hold values from -6 to 6
- value_image: bfloat16 [2048, 1024], P(('outer', 'inner')), may hold values from -6 to 6
- attended_image: bfloat16 [2048, 1024], P(('outer', 'inner')), may hold values from -6 to 6
- upstream_image: bfloat16 [2048, 1024], P(('outer', 'inner')), may hold values from -128 to 128
- logsum_image: float32 [2048, 8], P(('outer', 'inner')), may hold values from 8.6 to 9.4
- query_text: bfloat16 [512, 1024], P(None, 'outer'), may hold values from -6 to 6
- key_text: bfloat16 [512, 1024], P(None, 'outer'), may hold values from -6 to 6
- value_text: bfloat16 [512, 1024], P(None, 'outer'), may hold values from -6 to 6
- attended_text: bfloat16 [512, 1024], P(None, 'outer'), may hold values from -6 to 6
- upstream_text: bfloat16 [512, 1024], P(None, 'outer'), may hold values from -128 to 128
- logsum_text: float32 [512, 8], P(None, 'outer'), may hold values from 8.6 to 9.4
Outputs:
- grad_query_image: bfloat16 [2048, 1024], P(('outer', 'inner'))
- grad_key_image: bfloat16 [2048, 1024], P(('outer', 'inner'))
- grad_value_image: bfloat16 [2048, 1024], P(('outer', 'inner'))
- grad_query_text: bfloat16 [512, 1024], P('inner', 'outer')
- grad_key_text: bfloat16 [512, 1024], P('inner', 'outer')
- grad_value_text: bfloat16 [512, 1024], P('inner', 'outer')
The draws below stay inside these ranges and needn't reach their ends.
All inputs are finite; a program needn't handle non-finite values.
Results may differ from the reference program's by a relative error of at most 0.0055.
Values may be sent and summed in bfloat16 or wider, within the bound.
A program may use at most 64 MiB of HBM per device.

```python
import jax
import jax.numpy as jnp
from jax import lax

HEAD_DIM = 128
TEXT = 512
TOK_DEV = 512
HEADS = 8
IMAGE = 2048
WIDTH = 1024
N_INNER = 4


def block_scale(stream_key, extent, cuts, low, top_value):
    gain, own = 1.0, jax.random.fold_in(stream_key, 6)
    for dim, blocks in cuts:
        steps = jnp.exp(jax.random.uniform(jax.random.fold_in(own, dim), (blocks,), jnp.float32, low / len(cuts), top_value / len(cuts)))
        gain = gain * jnp.repeat(steps, extent[dim] // blocks).reshape([-1 if axis == dim else 1 for axis in range(len(extent))])
    return gain


def scatter_about(rng, shape, spread, bound, pieces=(), kind=jnp.bfloat16):
    values = jax.random.normal(rng, shape, jnp.float32) * spread
    if len(pieces) > 0:
        values = block_scale(rng, shape, pieces, -0.22, 0.18) * values
    return jnp.clip(values, min=-bound, max=bound).astype(kind)


def setup_inputs(seed: int = 0) -> dict:
    key_of = jax.random.split(jax.random.key(seed), 13)
    return {
        "query_image": scatter_about(key_of[0], (IMAGE, WIDTH), 1.0, 6.0, ((0, 32),)),
        "key_image": scatter_about(key_of[1], (IMAGE, WIDTH), 1.0, 6.0, ((0, 32),)),
        "value_image": scatter_about(key_of[2], (IMAGE, WIDTH), 1.0, 6.0, ((0, 32),)),
        "attended_image": scatter_about(key_of[3], (IMAGE, WIDTH), 1.0, 6.0, ((0, 32),)),
        "upstream_image": scatter_about(key_of[4], (IMAGE, WIDTH), 24.0, 128.0, ((0, 32),)),
        "logsum_image": jnp.clip(8.6 + 0.79999924 * jax.random.uniform(key_of[5], (IMAGE, HEADS), jnp.float32) ** block_scale(key_of[5], (IMAGE, HEADS), ((0, 32),), -0.2, 0.2), 8.6, 9.4),
        "query_text": scatter_about(key_of[6], (TEXT, WIDTH), 1.0, 6.0, ((1, 8),)),
        "key_text": scatter_about(key_of[7], (TEXT, WIDTH), 1.0, 6.0, ((1, 8),)),
        "value_text": scatter_about(key_of[8], (TEXT, WIDTH), 1.0, 6.0, ((1, 8),)),
        "attended_text": scatter_about(key_of[9], (TEXT, WIDTH), 1.0, 6.0, ((1, 8),)),
        "upstream_text": scatter_about(key_of[10], (TEXT, WIDTH), 24.0, 128.0, ((1, 8),)),
        "logsum_text": jnp.clip(8.6 + 0.79999924 * jax.random.uniform(key_of[11], (TEXT, HEADS), jnp.float32) ** block_scale(key_of[11], (TEXT, HEADS), ((1, 8),), -0.2, 0.2), 8.6, 9.4),
    }


def weights_and_mixed(queries, upstream, log_sums, deltas, keys, values):
    scores = jnp.dot(queries, keys.T, preferred_element_type=jnp.float32) * (HEAD_DIM ** -0.5)
    weights = jnp.exp(scores - log_sums)
    slopes = jnp.dot(upstream, values.T, preferred_element_type=jnp.float32)
    mixed = weights * (slopes - deltas)
    return weights.astype(jnp.bfloat16), mixed.astype(jnp.bfloat16)


def query_side(mixed_half, keys):
    return jnp.dot(mixed_half, keys, preferred_element_type=jnp.float32) * (HEAD_DIM ** -0.5)


def key_side(weights_half, mixed_half, queries, upstream):
    grad_values = jnp.dot(weights_half.T, upstream, preferred_element_type=jnp.float32)
    grad_keys = jnp.dot(mixed_half.T, queries, preferred_element_type=jnp.float32) * (HEAD_DIM ** -0.5)
    return grad_keys, grad_values


def reference(query_image, key_image, value_image, attended_image, upstream_image, logsum_image,
              query_text, key_text, value_text, attended_text, upstream_text, logsum_text):
    queries = jnp.concatenate([query_text, query_image], axis=0)
    keys = jnp.concatenate([key_text, key_image], axis=0)
    values = jnp.concatenate([value_text, value_image], axis=0)
    attended = jnp.concatenate([attended_text, attended_image], axis=0)
    upstream = jnp.concatenate([upstream_text, upstream_image], axis=0)
    log_sums = jnp.concatenate([logsum_text, logsum_image], axis=0)
    total = TEXT + IMAGE

    def one_head(head):
        start = head * HEAD_DIM

        def columns(matrix):
            return lax.dynamic_slice_in_dim(matrix, start, HEAD_DIM, 1)

        head_q = columns(queries)
        head_k = columns(keys)
        head_v = columns(values)
        head_g = columns(upstream)
        head_o = columns(attended)
        head_l = lax.dynamic_slice_in_dim(log_sums, head, 1, 1)
        head_delta = jnp.sum(head_g.astype(jnp.float32) * head_o.astype(jnp.float32), axis=1, keepdims=True)
        empty = jnp.zeros((total, HEAD_DIM), jnp.float32)

        def block_back(carry, block):
            block_q, block_g, block_l, block_d = block
            weights_half, mixed_half = weights_and_mixed(block_q, block_g, block_l, block_d, head_k, head_v)
            grad_q = query_side(mixed_half, head_k)
            grad_k, grad_v = key_side(weights_half, mixed_half, block_q, block_g)
            return (carry[0] + grad_k, carry[1] + grad_v), grad_q

        carry, text_q = block_back((empty, empty), (head_q[:TEXT], head_g[:TEXT], head_l[:TEXT], head_delta[:TEXT]))
        blocks = tuple(item[TEXT:].reshape((N_INNER, TOK_DEV) + item.shape[1:])
                       for item in (head_q, head_g, head_l, head_delta))
        (grad_k, grad_v), image_q = lax.scan(block_back, carry, blocks)
        grad_q = jnp.concatenate([text_q, image_q.reshape(IMAGE, HEAD_DIM)], axis=0)
        return grad_q, grad_k, grad_v

    grad_q, grad_k, grad_v = lax.map(one_head, jnp.arange(HEADS, dtype=jnp.int32))

    def join_heads(stacked):
        return jnp.transpose(stacked, (1, 0, 2)).reshape(total, HEADS * HEAD_DIM).astype(jnp.bfloat16)

    grad_q = join_heads(grad_q)
    grad_k = join_heads(grad_k)
    grad_v = join_heads(grad_v)
    return (grad_q[TEXT:], grad_k[TEXT:], grad_v[TEXT:],
            grad_q[:TEXT], grad_k[:TEXT], grad_v[:TEXT])
```

```python
import functools
import math

import jax
import jax.numpy as jnp
from jax import lax
from jax.experimental import pallas as pl
from jax.experimental.pallas import tpu as pltpu
from jax.sharding import PartitionSpec as P

HEAD_DIM = 128
LANES = 128
MESH = pl.DeviceIdType.MESH


def across_rows(left, right, **options):
    return lax.dot_general(
        left, right, (((1,), (1,)), ((), ())), preferred_element_type=jnp.float32, **options
    )


def ring_digits(n_out):
    cores = 2 if n_out % 2 == 0 else 1
    chips = 2 if n_out // cores % 2 == 0 else 1
    return cores, chips


def kernel(
    dims,
    q_ref, k_ref, v_ref, o_ref, g_ref, l_ref,
    qt_ref, kt_ref, vt_ref, ot_ref, gt_ref, lt_ref,
    out_q, out_k, out_v, out_qt, out_kt, out_vt,
    qg, kv, key_flip, lines_in, stat_send, stat, row_stat, own_o, staged, text_o,
    dq_acc, dkv_acc, dq_send, dq_recv, dkv_send, dkv_recv, final,
    local_sem, text_sem, in_send, in_recv, gather_send, gather_recv,
    sum_send, sum_recv, out_send, out_recv,
):
    n_out, n_in, rows, columns, tokens, block, share = dims
    span = block + share
    d = HEAD_DIM
    scale = HEAD_DIM ** (-0.5)
    o = lax.axis_index("outer")
    i = lax.axis_index("inner")

    line, place_in = i // rows, i % rows

    def row_peer(a):
        return (line + a) % columns * rows + place_in

    def column_peer(b):
        return line * rows + (place_in + b) % rows

    cores, chips = ring_digits(n_out)
    core, chip, far = o % cores, o // cores % chips, o // (cores * chips)

    def stepped(k, sign):
        core_step, chip_step, far_step = k % cores, k // cores % chips, k // (cores * chips)
        groups = n_out // (cores * chips)
        there = (far + sign * far_step + groups) % groups * chips
        there = (there + (chip + sign * chip_step + chips) % chips) * cores
        return there + (core + sign * core_step + cores) % cores

    def other(k):
        return stepped(k, 1)

    def hops(k):
        return (k // cores % chips > 0) + (k // (cores * chips) > 0), k % cores, k

    relayed = sorted(range(cores, n_out), key=hops)

    own_loads = [
        pltpu.make_async_copy(k_ref, staged.at[0, 0], local_sem.at[0]),
        pltpu.make_async_copy(v_ref, staged.at[0, 1], local_sem.at[1]),
        pltpu.make_async_copy(q_ref, staged.at[1, 0], local_sem.at[2]),
        pltpu.make_async_copy(g_ref, staged.at[1, 1], local_sem.at[3]),
        pltpu.make_async_copy(o_ref, own_o, local_sem.at[4]),
    ]
    for copy in own_loads:
        copy.start()

    barrier = pltpu.get_barrier_semaphore()
    for k in range(1, n_out):
        pl.semaphore_signal(barrier, inc=1, device_id=(other(k), i), device_id_type=MESH)
    for k in range(cores):
        for a in range(1, columns):
            pl.semaphore_signal(barrier, inc=1, device_id=(other(k), row_peer(a)), device_id_type=MESH)
        for b in range(1, rows):
            pl.semaphore_signal(barrier, inc=1, device_id=(other(k), column_peer(b)), device_id_type=MESH)

    text_loads = []

    def text_load(source, peer, target):
        copy = pltpu.make_async_copy(
            source.at[pl.ds(pl.multiple_of(peer * share, share), share)],
            target,
            text_sem.at[len(text_loads)],
        )
        copy.start()
        text_loads.append(copy)

    text = pl.ds(block, share)
    for b in range(rows):
        text_load(kt_ref, column_peer(b), kv.at[b, 0, text])
        text_load(vt_ref, column_peer(b), kv.at[b, 1, text])
    for a in range(columns):
        text_load(qt_ref, row_peer(a), qg.at[a, 0, text])
        text_load(gt_ref, row_peer(a), qg.at[a, 1, text])
        text_load(ot_ref, row_peer(a), text_o.at[a])

    pl.semaphore_wait(barrier, n_out - 1 + cores * (columns - 1 + rows - 1))

    def piece(k):
        return pl.ds(k * tokens, tokens)

    def exchange(which, source, target, k):
        if k == 0:
            return pltpu.make_async_copy(source, target, in_recv.at[which, 0])
        return pltpu.make_async_remote_copy(
            src_ref=source,
            dst_ref=target,
            send_sem=in_send.at[which, k],
            recv_sem=in_recv.at[which, k],
            device_id=(other(k), i),
            device_id_type=MESH,
        )

    def head_of(which, k):
        return staged.at[which, :, :, pl.ds(pl.multiple_of(other(k) * d, d), d)]

    homes = (kv, qg)
    sizes = (rows, columns, columns)

    def arrival(which, k):
        if which == 2:
            return exchange(2, stat_send.at[other(k)], stat.at[0, k], k)
        return exchange(which, head_of(which, k), homes[which].at[0, :, piece(k)], k)

    def gather(which, offset, k):
        place = (sizes[which] - offset) % sizes[which]
        if which == 2:
            source, target = stat.at[0], stat.at[place]
        else:
            source = head_of(which, k) if k < cores else homes[which].at[0, :, piece(k)]
            target = homes[which].at[place, :, piece(k)]
        peer = row_peer(offset) if which else column_peer(offset)
        return pltpu.make_async_remote_copy(
            src_ref=source,
            dst_ref=target,
            send_sem=gather_send.at[which, offset, k],
            recv_sem=gather_recv.at[which, place, k],
            device_id=(other(k) if which < 2 and k < cores else o, peer),
            device_id_type=MESH,
        )

    at_end = jnp.logical_or(i == 0, i == n_in - 1)

    def ordered(first, second):
        @pl.when(at_end)
        def _():
            first()
            second()

        @pl.when(jnp.logical_not(at_end))
        def _():
            second()
            first()

    def depart(which):
        for k in range(cores):
            for offset in range(1, sizes[which]):
                gather(which, offset, k).start()
        for k in relayed + list(range(cores)):
            arrival(which, k).start()

    for copy in own_loads:
        copy.wait()
    ordered(lambda: depart(0), lambda: depart(1))

    lane = lax.broadcasted_iota(jnp.int32, (1, LANES), 1)
    ones = jnp.ones((8, d), jnp.float32)
    repeats = LANES // tokens
    lines_in[...] = jnp.zeros_like(lines_in)
    lines_in[:, 0:tokens] = l_ref[...]
    image_lines = lines_in[...]
    for p in range(1, repeats):
        moved = pltpu.roll(lines_in[...], p * tokens, 1)
        image_lines = jnp.where(lane // tokens == p, moved, image_lines)
    for h in range(n_out):
        cut = slice(h * d, (h + 1) * d)
        product = staged[1, 1, :, cut].astype(jnp.float32) * own_o[:, cut].astype(jnp.float32)
        product = jnp.concatenate([product] * repeats, axis=0)
        delta = across_rows(ones, product, precision=lax.Precision.HIGHEST)
        stat_send[h, 0:1, :] = image_lines[h : h + 1, :]
        stat_send[h, 1:2, :] = delta[0:1, :]
    for k in range(n_out):
        arrival(2, k).start()

    def landed(which, k):
        if k == 0:
            arrival(which, k).wait()
        else:
            arrival(which, k).wait_recv()

    def forward(which):
        for k in relayed:
            landed(which, k)
            for offset in range(1, sizes[which]):
                gather(which, offset, k).start()

    ordered(lambda: forward(0), lambda: forward(1))
    for which in range(2):
        for k in range(cores):
            landed(which, k)
    for k in range(n_out):
        landed(2, k)
    for offset in range(1, columns):
        gather(2, offset, 0).start()

    for copy in text_loads:
        copy.wait()
    for a in range(columns):
        product = qg[a, 1, text].astype(jnp.float32) * text_o[a].astype(jnp.float32)
        delta = across_rows(ones, product, precision=lax.Precision.HIGHEST)
        row_stat[a, 0:1, text] = lt_ref[row_peer(a)]
        row_stat[a, 1:2, text] = delta[0:1, :]

    dq_acc[...] = jnp.zeros_like(dq_acc)
    dkv_acc[...] = jnp.zeros_like(dkv_acc)

    def spread_statistics(a):
        for start in range(0, block, LANES):
            first = start // tokens
            lines = [stat[a, first + p] for p in range(min(repeats, n_out - first))]
            merged = lines[0]
            for p in range(1, len(lines)):
                merged = jnp.where(lane // tokens == p, lines[p], merged)
            row_stat[a, :, start : start + LANES] = merged

    def flip_keys(b):
        key_flip[b] = kv[b, 0].astype(jnp.float32).T.astype(jnp.bfloat16)

    size = math.gcd(block, 256)
    chunks = [(start, size) for start in range(0, block, size)] + [(block, share)]
    halves = [(0, size), (size, span - size)]

    def total(kind, offset, n):
        group = rows if kind else columns
        place = (group - offset) % group
        start, length = (halves if kind else chunks)[n]
        cut = pl.ds(start, length)
        if kind:
            source, target = dkv_send.at[offset, kind - 1, cut], dkv_recv.at[place, kind - 1, cut]
        else:
            source, target = dq_send.at[offset, cut], dq_recv.at[place, cut]
        peer = column_peer(offset) if kind else row_peer(offset)
        return pltpu.make_async_remote_copy(
            src_ref=source,
            dst_ref=target,
            send_sem=sum_send.at[kind, offset, n],
            recv_sem=sum_recv.at[kind, place, n],
            device_id=(o, peer),
            device_id_type=MESH,
        )

    def query_sum(a, n):
        start, length = chunks[n]
        return dq_acc[a, :, start : start + length].T * scale

    def work(a, b, n):
        start, length = chunks[n]
        cut = slice(start, start + length)
        keys, values = kv[b, 0], kv[b, 1]
        queries, upstream = qg[a, 0, cut], qg[a, 1, cut]
        scores = across_rows(keys, queries) * scale
        weights = jnp.exp(scores - row_stat[a, 0:1, cut])
        slopes = across_rows(values, upstream)
        mixed = (weights * (slopes - row_stat[a, 1:2, cut])).astype(jnp.bfloat16)
        weights = weights.astype(jnp.bfloat16)
        dkv_acc[b, 1] += jnp.dot(weights, upstream, preferred_element_type=jnp.float32)
        dkv_acc[b, 0] += jnp.dot(mixed, queries, preferred_element_type=jnp.float32)
        dq_acc[a, :, cut] += jnp.dot(key_flip[b], mixed, preferred_element_type=jnp.float32)

    spread_statistics(0)
    flip_keys(0)
    for n in range(len(chunks)):
        work(0, 0, n)

    def near_keys_landed(b):
        for k in range(n_out):
            gather(0, (rows - b) % rows, k).wait_recv()
        flip_keys(b)

    def far_queries_landed(a, n):
        start, length = chunks[n]
        if start < block:
            for k in range(start // tokens, (start + length) // tokens):
                gather(1, (columns - a) % columns, k).wait_recv()
        if start == 0:
            gather(2, (columns - a) % columns, 0).wait_recv()
            spread_statistics(a)

    def send_queries(a, n):
        start, length = chunks[n]
        dq_send[a, start : start + length] = query_sum(a, n).astype(jnp.bfloat16)
        total(0, a, n).start()

    def send_keys(b):
        for part in (0, 1):
            for n, (start, length) in enumerate(halves):
                cut = slice(start, start + length)
                grad = dkv_acc[b, part, cut]
                if part == 0:
                    grad = grad * scale
                dkv_send[b, part, cut] = grad.astype(jnp.bfloat16)
                total(1 + part, b, n).start()

    places = (len(chunks) - 1, *range(len(chunks) - 1))

    def loop(first, last, body):
        def with_carry(index, carry):
            body(index)
            return carry

        lax.fori_loop(first, last, with_carry, 0)

    @pl.when(jnp.logical_not(at_end))
    def _():
        def near_keys(b):
            near_keys_landed(b)
            for n in places:
                work(0, b, n)

        def far_queries(a):
            for n in places:
                far_queries_landed(a, n)
                loop(0, rows, lambda b: work(a, b, n))
                send_queries(a, n)

        loop(1, rows, near_keys)
        loop(1, columns, far_queries)
        loop(1, rows, send_keys)

    @pl.when(at_end)
    def _():
        def far_queries(a):
            for n in places:
                far_queries_landed(a, n)
                work(a, 0, n)

        def near_keys(b):
            near_keys_landed(b)

            def with_queries(a):
                for n in places:
                    work(a, b, n)

            loop(0, columns, with_queries)
            send_keys(b)

        def give_queries(a):
            for n in places:
                send_queries(a, n)

        loop(1, columns, far_queries)
        loop(1, rows, near_keys)
        loop(1, columns, give_queries)

    mine = pl.ds(pl.multiple_of(o * d, d), d)
    images, texts = (out_q, out_k, out_v), (out_qt, out_kt, out_vt)

    def out_copy(which, k):
        source, target = final.at[which, piece(k)], images[which].at[:, mine]
        if k == 0:
            return pltpu.make_async_copy(source, target, out_recv.at[which, 0])
        return pltpu.make_async_remote_copy(
            src_ref=source,
            dst_ref=target,
            send_sem=out_send.at[which, k],
            recv_sem=out_recv.at[which, k],
            device_id=(stepped(k, -1), i),
            device_id_type=MESH,
        )

    def text_copy(which):
        return pltpu.make_async_copy(final.at[which, text], texts[which], out_send.at[which, 0])

    def give_back(which, start, length):
        for k in range(start // tokens, min(start + length, block) // tokens):
            out_copy(which, k).start()
        if start + length == span:
            text_copy(which).start()

    def finish_queries():
        for n in places:
            start, length = chunks[n]
            cut = slice(start, start + length)
            grad = query_sum(0, n)
            for a in range(1, columns):
                total(0, (columns - a) % columns, n).wait_recv()
                grad = grad + dq_recv[a, cut].astype(jnp.float32)
            final[0, cut] = grad.astype(jnp.bfloat16)
            give_back(0, start, length)

    def finish_keys():
        for part in (0, 1):
            for n, (start, length) in enumerate(halves):
                cut = slice(start, start + length)
                grad = dkv_acc[0, part, cut]
                if part == 0:
                    grad = grad * scale
                for b in range(1, rows):
                    total(1 + part, (rows - b) % rows, n).wait_recv()
                    grad = grad + dkv_recv[b, part, cut].astype(jnp.float32)
                final[1 + part, cut] = grad.astype(jnp.bfloat16)
                give_back(1 + part, start, length)

    ordered(finish_queries, finish_keys)

    for which in range(3):
        for k in range(1, n_out):
            arrival(which, k).wait_send()
    for which in range(2):
        for offset in range(1, sizes[which]):
            for k in range(n_out):
                gather(which, offset, k).wait_send()
    for a in range(1, columns):
        gather(2, a, 0).wait_send()
        for n in range(len(chunks)):
            total(0, a, n).wait_send()
    for b in range(1, rows):
        for n in range(len(halves)):
            total(1, b, n).wait_send()
            total(2, b, n).wait_send()
    for which in range(3):
        text_copy(which).wait()
        for k in range(n_out):
            out_copy(which, k).wait()


def tail(*refs):
    sources, targets, held = refs[:6], refs[6:12], refs[12:18]
    sem = refs[18]
    loads = [pltpu.make_async_copy(s, h, sem.at[0, n]) for n, (s, h) in enumerate(zip(sources, held))]
    stores = [pltpu.make_async_copy(h, t, sem.at[1, n]) for n, (h, t) in enumerate(zip(held, targets))]
    for load in loads:
        load.start()
    for load, store in zip(loads, stores):
        load.wait()
        store.start()
    for store in stores:
        store.wait()


def shards(
    mesh,
    query_image,
    key_image,
    value_image,
    attended_image,
    upstream_image,
    logsum_image,
    query_text,
    key_text,
    value_text,
    attended_text,
    upstream_text,
    logsum_text,
):
    n_out, n_in = mesh.shape["outer"], mesh.shape["inner"]
    rows = max(c for c in range(1, math.isqrt(n_in) + 1) if n_in % c == 0)
    columns = n_in // rows
    tokens, width = query_image.shape
    block = tokens * n_out
    share = query_text.shape[0] // n_in
    span = block + share
    d = HEAD_DIM
    text_lines = logsum_text.reshape(n_in, 1, share)
    half, full = jnp.bfloat16, jnp.float32
    dma = pltpu.SemaphoreType.DMA
    vmem = pl.BlockSpec(memory_space=pltpu.VMEM)
    hbm = pl.BlockSpec(memory_space=pl.ANY)
    image_out = jax.ShapeDtypeStruct((tokens, width), half)
    text_out = jax.ShapeDtypeStruct((share, d), half)
    grads = pl.pallas_call(
        functools.partial(kernel, (n_out, n_in, rows, columns, tokens, block, share)),
        out_shape=(image_out,) * 3 + (text_out,) * 3,
        in_specs=[hbm] * 5 + [vmem] + [hbm] * 5 + [vmem],
        out_specs=(hbm,) * 6,
        scratch_shapes=[
            pltpu.VMEM((columns, 2, span, d), half),
            pltpu.VMEM((rows, 2, span, d), half),
            pltpu.VMEM((rows, d, span), half),
            pltpu.VMEM((n_out, LANES), full),
            pltpu.VMEM((n_out, 2, LANES), full),
            pltpu.VMEM((columns, n_out, 2, LANES), full),
            pltpu.VMEM((columns, 2, span), full),
            pltpu.VMEM((tokens, width), half),
            pltpu.VMEM((2, 2, tokens, width), half),
            pltpu.VMEM((columns, share, d), half),
            pltpu.VMEM((columns, d, span), full),
            pltpu.VMEM((rows, 2, span, d), full),
            pltpu.VMEM((columns, span, d), half),
            pltpu.VMEM((columns, span, d), half),
            pltpu.VMEM((rows, 2, span, d), half),
            pltpu.VMEM((rows, 2, span, d), half),
            pltpu.VMEM((3, span, d), half),
            dma((5,)),
            dma((2 * rows + 3 * columns,)),
            dma((3, n_out)),
            dma((3, n_out)),
            dma((3, max(rows, columns), n_out)),
            dma((3, max(rows, columns), n_out)),
            dma((3, max(rows, columns), 1 + block // math.gcd(block, 256))),
            dma((3, max(rows, columns), 1 + block // math.gcd(block, 256))),
            dma((3, n_out)),
            dma((3, n_out)),
        ],
        compiler_params=pltpu.CompilerParams(collective_id=0, has_side_effects=True),
    )(
        query_image, key_image, value_image, attended_image, upstream_image, logsum_image.T,
        query_text, key_text, value_text, attended_text, upstream_text, text_lines,
    )
    return pl.pallas_call(
        tail,
        out_shape=(image_out,) * 3 + (text_out,) * 3,
        in_specs=[hbm] * 6,
        out_specs=(hbm,) * 6,
        scratch_shapes=[pltpu.VMEM((tokens, width), half)] * 3
        + [pltpu.VMEM((share, d), half)] * 3
        + [dma((2, 6))],
    )(*grads)


def solution(mesh):
    tokens_spec = P(("outer", "inner"), None)
    return jax.shard_map(
        functools.partial(shards, mesh),
        mesh=mesh,
        in_specs=(tokens_spec,) * 6 + (P(None, "outer"),) * 6,
        out_specs=(tokens_spec,) * 3 + (P("inner", "outer"),) * 3,
        check_vma=False,
    )
```

```python
import functools
import math

import jax
import jax.numpy as jnp
from jax import lax
from jax.experimental import pallas as pl
from jax.experimental.pallas import tpu as pltpu
from jax.sharding import PartitionSpec as P

HEAD_DIM = 128
LANES = 128
MESH = pl.DeviceIdType.MESH


def across_rows(left, right, **options):
    return lax.dot_general(
        left, right, (((1,), (1,)), ((), ())), preferred_element_type=jnp.float32, **options
    )


def ring_steps(n_out):
    cores = 2 if n_out % 2 == 0 else 1
    chips = 2 if n_out // cores % 2 == 0 else 1
    steps = [
        (far, chip, core)
        for far in range(n_out // (cores * chips))
        for chip in range(chips)
        for core in range(cores)
    ]
    return cores, chips, sorted(steps, key=lambda s: ((s[0] > 0) + (s[1] > 0), s[2] if s[0] + s[1] else 0, s))


def kernel(
    dims,
    q_ref, k_ref, v_ref, o_ref, g_ref, l_ref,
    qt_ref, kt_ref, vt_ref, ot_ref, gt_ref, lt_ref,
    out_q, out_k, out_v, out_qt, out_kt, out_vt,
    qg, kv, key_flip, lines_in, stat_send, stat, row_stat, own_o, staged, text_o,
    dq_acc, dkv_acc, dq_own, dq_send, dq_recv, dkv_send, dkv_recv, final,
    local_sem, text_sem, in_send, in_recv, gather_send, gather_recv,
    sum_send, sum_recv, out_send, out_recv, out_local,
):
    n_out, n_in, rows, columns, tokens, block, share = dims
    span = block + share
    d = HEAD_DIM
    scale = HEAD_DIM ** (-0.5)
    o = lax.axis_index("outer")
    i = lax.axis_index("inner")

    line, place_in = i // rows, i % rows

    def row_peer(a):
        return (line + a) % columns * rows + place_in

    def column_peer(b):
        return line * rows + (place_in + b) % rows

    cores, chips, steps = ring_steps(n_out)
    core, chip, far = o % cores, o // cores % chips, o // (cores * chips)

    def stepped(k, sign):
        far_step, chip_step, core_step = steps[k]
        groups = n_out // (cores * chips)
        there = (far + sign * far_step + groups) % groups * chips
        there = (there + (chip + sign * chip_step + chips) % chips) * cores
        return there + (core + sign * core_step + cores) % cores

    def other(k):
        return stepped(k, 1)

    own_loads = [
        pltpu.make_async_copy(k_ref, staged.at[0, 0], local_sem.at[0]),
        pltpu.make_async_copy(v_ref, staged.at[0, 1], local_sem.at[1]),
        pltpu.make_async_copy(q_ref, staged.at[1, 0], local_sem.at[2]),
        pltpu.make_async_copy(g_ref, staged.at[1, 1], local_sem.at[3]),
        pltpu.make_async_copy(o_ref, own_o, local_sem.at[4]),
    ]
    for copy in own_loads:
        copy.start()

    barrier = pltpu.get_barrier_semaphore()
    for k in range(1, n_out):
        pl.semaphore_signal(barrier, inc=1, device_id=(other(k), i), device_id_type=MESH)
    for k in range(cores):
        for a in range(1, columns):
            pl.semaphore_signal(barrier, inc=1, device_id=(other(k), row_peer(a)), device_id_type=MESH)
        for b in range(1, rows):
            pl.semaphore_signal(barrier, inc=1, device_id=(other(k), column_peer(b)), device_id_type=MESH)

    text_loads = []

    def text_load(source, peer, target):
        copy = pltpu.make_async_copy(
            source.at[pl.ds(pl.multiple_of(peer * share, share), share)],
            target,
            text_sem.at[len(text_loads)],
        )
        copy.start()
        text_loads.append(copy)

    text = pl.ds(block, share)
    for b in range(rows):
        text_load(kt_ref, column_peer(b), kv.at[b, 0, text])
        text_load(vt_ref, column_peer(b), kv.at[b, 1, text])
    for a in range(columns):
        text_load(qt_ref, row_peer(a), qg.at[a, 0, text])
        text_load(gt_ref, row_peer(a), qg.at[a, 1, text])
        text_load(ot_ref, row_peer(a), text_o.at[a])

    pl.semaphore_wait(barrier, n_out - 1 + cores * (columns - 1 + rows - 1))

    def piece(k):
        return pl.ds(k * tokens, tokens)

    def exchange(which, source, target, k):
        if k == 0:
            return pltpu.make_async_copy(source, target, in_recv.at[which, 0])
        return pltpu.make_async_remote_copy(
            src_ref=source,
            dst_ref=target,
            send_sem=in_send.at[which, k],
            recv_sem=in_recv.at[which, k],
            device_id=(other(k), i),
            device_id_type=MESH,
        )

    def head_of(which, k):
        return staged.at[which, :, :, pl.ds(pl.multiple_of(other(k) * d, d), d)]

    homes = (kv, qg)
    sizes = (rows, columns, columns)

    def arrival(which, k):
        if which == 2:
            return exchange(2, stat_send.at[other(k)], stat.at[0, k], k)
        return exchange(which, head_of(which, k), homes[which].at[0, :, piece(k)], k)

    def gather(which, offset, k):
        place = (sizes[which] - offset) % sizes[which]
        if which == 2:
            source, target = stat.at[0], stat.at[place]
        else:
            source = head_of(which, k) if k < cores else homes[which].at[0, :, piece(k)]
            target = homes[which].at[place, :, piece(k)]
        peer = row_peer(offset) if which else column_peer(offset)
        return pltpu.make_async_remote_copy(
            src_ref=source,
            dst_ref=target,
            send_sem=gather_send.at[which, offset, k],
            recv_sem=gather_recv.at[which, place, k],
            device_id=(other(k) if which < 2 and k < cores else o, peer),
            device_id_type=MESH,
        )

    at_end = jnp.logical_or(i == 0, i == n_in - 1)

    def ordered(first, second):
        @pl.when(at_end)
        def _():
            first()
            second()

        @pl.when(jnp.logical_not(at_end))
        def _():
            second()
            first()

    def depart(which):
        for k in range(cores):
            for offset in range(1, sizes[which]):
                gather(which, offset, k).start()
        for k in (*range(cores, n_out), *range(cores)):
            arrival(which, k).start()

    for copy in own_loads:
        copy.wait()
    ordered(lambda: depart(0), lambda: depart(1))

    lane = lax.broadcasted_iota(jnp.int32, (1, LANES), 1)
    ones = jnp.ones((8, d), jnp.float32)
    repeats = LANES // tokens
    lines_in[...] = jnp.zeros_like(lines_in)
    lines_in[:, 0:tokens] = l_ref[...]
    image_lines = lines_in[...]
    for p in range(1, repeats):
        moved = pltpu.roll(lines_in[...], p * tokens, 1)
        image_lines = jnp.where(lane // tokens == p, moved, image_lines)
    for h in range(n_out):
        cut = slice(h * d, (h + 1) * d)
        product = staged[1, 1, :, cut].astype(jnp.float32) * own_o[:, cut].astype(jnp.float32)
        product = jnp.concatenate([product] * repeats, axis=0)
        delta = across_rows(ones, product, precision=lax.Precision.HIGHEST)
        stat_send[h, 0:1, :] = image_lines[h : h + 1, :]
        stat_send[h, 1:2, :] = delta[0:1, :]
    for k in range(n_out):
        arrival(2, k).start()

    def landed(which, k):
        if k == 0:
            arrival(which, k).wait()
        else:
            arrival(which, k).wait_recv()

    def forward(which):
        for k in range(cores, n_out):
            landed(which, k)
            for offset in range(1, sizes[which]):
                gather(which, offset, k).start()

    ordered(lambda: forward(0), lambda: forward(1))
    for which in range(2):
        for k in range(cores):
            landed(which, k)
    for k in range(n_out):
        landed(2, k)
    for offset in range(1, columns):
        gather(2, offset, 0).start()

    for copy in text_loads:
        copy.wait()
    for a in range(columns):
        product = qg[a, 1, text].astype(jnp.float32) * text_o[a].astype(jnp.float32)
        delta = across_rows(ones, product, precision=lax.Precision.HIGHEST)
        row_stat[a, 0:1, text] = lt_ref[row_peer(a)]
        row_stat[a, 1:2, text] = delta[0:1, :]

    dq_acc[...] = jnp.zeros_like(dq_acc)
    dkv_acc[...] = jnp.zeros_like(dkv_acc)

    def spread_statistics(a):
        for start in range(0, block, LANES):
            first = start // tokens
            lines = [stat[a, first + p] for p in range(min(repeats, n_out - first))]
            merged = lines[0]
            for p in range(1, len(lines)):
                merged = jnp.where(lane // tokens == p, lines[p], merged)
            row_stat[a, :, start : start + LANES] = merged

    def flip_keys(b):
        key_flip[b] = kv[b, 0].astype(jnp.float32).T.astype(jnp.bfloat16)

    size = math.gcd(block, 256)
    chunks = [(start, size) for start in range(0, block, size)] + [(block, share)]

    def total(kind, offset, n):
        group = rows if kind else columns
        place = (group - offset) % group
        cut = piece(n) if n < n_out else text
        if kind:
            source, target = dkv_send.at[offset, :, cut], dkv_recv.at[place, :, cut]
        else:
            source, target = dq_send.at[offset, cut], dq_recv.at[place, cut]
        peer = column_peer(offset) if kind else row_peer(offset)
        return pltpu.make_async_remote_copy(
            src_ref=source,
            dst_ref=target,
            send_sem=sum_send.at[kind, offset, n],
            recv_sem=sum_recv.at[kind, place, n],
            device_id=(o, peer),
            device_id_type=MESH,
        )

    def pieces(n):
        start, length = chunks[n]
        return range(start // tokens, (start + length) // tokens) if start < block else (n_out,)

    def query_sum(a, n):
        start, length = chunks[n]
        return dq_acc[a, :, start : start + length].T * scale

    def work(a, b, n):
        start, length = chunks[n]
        cut = slice(start, start + length)
        keys, values = kv[b, 0], kv[b, 1]
        queries, upstream = qg[a, 0, cut], qg[a, 1, cut]
        scores = across_rows(keys, queries) * scale
        weights = jnp.exp(scores - row_stat[a, 0:1, cut])
        slopes = across_rows(values, upstream)
        mixed = (weights * (slopes - row_stat[a, 1:2, cut])).astype(jnp.bfloat16)
        weights = weights.astype(jnp.bfloat16)
        dkv_acc[b, 1] += jnp.dot(weights, upstream, preferred_element_type=jnp.float32)
        dkv_acc[b, 0] += jnp.dot(mixed, queries, preferred_element_type=jnp.float32)
        dq_acc[a, :, cut] += jnp.dot(key_flip[b], mixed, preferred_element_type=jnp.float32)

    def work_keys(a, b, n):
        start, length = chunks[n]
        cut = slice(start, start + length)
        keys, values = kv[b, 0, cut], kv[b, 1, cut]
        queries, upstream = qg[a, 0], qg[a, 1]
        scores = across_rows(keys, queries) * scale
        weights = jnp.exp(scores - row_stat[a, 0:1])
        slopes = across_rows(values, upstream)
        mixed = (weights * (slopes - row_stat[a, 1:2])).astype(jnp.bfloat16)
        weights = weights.astype(jnp.bfloat16)
        dkv_acc[b, 1, cut] += jnp.dot(weights, upstream, preferred_element_type=jnp.float32)
        dkv_acc[b, 0, cut] += jnp.dot(mixed, queries, preferred_element_type=jnp.float32)
        dq_acc[a] += jnp.dot(key_flip[b, :, cut], mixed, preferred_element_type=jnp.float32)

    spread_statistics(0)
    flip_keys(0)
    for n in range(len(chunks)):
        work(0, 0, n)

    def near_keys_landed(b, n):
        start, length = chunks[n]
        if start < block:
            for k in range(start // tokens, (start + length) // tokens):
                gather(0, (rows - b) % rows, k).wait_recv()
        cut = slice(start, start + length)
        key_flip[b, :, cut] = kv[b, 0, cut].astype(jnp.float32).T.astype(jnp.bfloat16)

    def far_queries_landed(a, n):
        start, length = chunks[n]
        if start < block:
            for k in range(start // tokens, (start + length) // tokens):
                gather(1, (columns - a) % columns, k).wait_recv()
        if start == 0:
            gather(2, (columns - a) % columns, 0).wait_recv()
            spread_statistics(a)

    def gathers_left(which):
        for offset in range(1, sizes[which]):
            for k in range(n_out):
                gather(which, offset, k).wait_send()

    def send_queries(a, n):
        start, length = chunks[n]
        dq_send[a, start : start + length] = query_sum(a, n).astype(jnp.bfloat16)
        for p in pieces(n):
            total(0, a, p).start()

    def send_keys(b, n):
        start, length = chunks[n]
        cut = slice(start, start + length)
        dkv_send[b, 0, cut] = (dkv_acc[b, 0, cut] * scale).astype(jnp.bfloat16)
        dkv_send[b, 1, cut] = dkv_acc[b, 1, cut].astype(jnp.bfloat16)
        for p in pieces(n):
            total(1, b, p).start()

    places = (len(chunks) - 1, *range(len(chunks) - 1))

    def loop(first, last, body):
        def with_carry(index, carry):
            body(index)
            return carry

        lax.fori_loop(first, last, with_carry, 0)

    @pl.when(jnp.logical_not(at_end))
    def _():
        def near_keys(b):
            for n in places:
                near_keys_landed(b, n)
            for n in places:
                work(0, b, n)

        def far_queries(a):
            for n in places[:-1]:
                far_queries_landed(a, n)
                loop(0, rows, lambda b: work(a, rows - 1 - b, n))
                send_queries(a, n)

        def give_keys(b):
            for n in places:
                send_keys(b, n)

        def last_queries(a):
            n = places[-1]
            far_queries_landed(a, n)
            loop(1, rows, lambda b: work(a, b, n))

        def give_queries(a):
            work(a, 0, places[-1])
            send_queries(a, places[-1])

        loop(1, rows, near_keys)
        loop(1, columns, far_queries)
        loop(1, columns, last_queries)
        loop(1, rows, give_keys)
        loop(1, columns, give_queries)
        gathers_left(0)
        gathers_left(1)

    @pl.when(at_end)
    def _():
        def far_queries(a):
            for n in places:
                far_queries_landed(a, n)
                work(a, 0, n)

        def near_keys(b):
            for n in places:
                near_keys_landed(b, n)
                loop(0, columns, lambda a: work_keys(a, b, n))
                send_keys(b, n)

        def give_queries(a):
            for n in places:
                send_queries(a, n)

        loop(1, columns, far_queries)
        loop(1, rows, near_keys)
        loop(1, columns, give_queries)
        gathers_left(0)
        gathers_left(1)

    mine = pl.ds(pl.multiple_of(o * d, d), d)
    images, texts = (out_q, out_k, out_v), (out_qt, out_kt, out_vt)

    def out_copy(which, k):
        source, target = final.at[which, piece(k)], images[which].at[:, mine]
        if k == 0:
            return pltpu.make_async_copy(source, target, out_local.at[0, which])
        return pltpu.make_async_remote_copy(
            src_ref=source,
            dst_ref=target,
            send_sem=out_send.at[which],
            recv_sem=out_recv.at[which],
            device_id=(stepped(k, -1), i),
            device_id_type=MESH,
        )

    def text_copy(which):
        return pltpu.make_async_copy(final.at[which, text], texts[which], out_local.at[1, which])

    def give_back(which, p):
        if p < n_out:
            out_copy(which, p).start()
        else:
            text_copy(which).start()

    def finish_queries():
        for n in range(len(chunks)):
            start, length = chunks[n]
            dq_own[start : start + length] = query_sum(0, n)
        for n in places:
            for p in pieces(n):
                cut = piece(p) if p < n_out else text
                grad = dq_own[cut]
                for a in range(1, columns):
                    total(0, (columns - a) % columns, p).wait_recv()
                    grad = grad + dq_recv[a, cut].astype(jnp.float32)
                final[0, cut] = grad.astype(jnp.bfloat16)
                give_back(0, p)

    def finish_keys():
        for n in places:
            for p in pieces(n):
                cut = piece(p) if p < n_out else text
                for b in range(1, rows):
                    total(1, (rows - b) % rows, p).wait_recv()
                for part in (0, 1):
                    grad = dkv_acc[0, part, cut]
                    if part == 0:
                        grad = grad * scale
                    for b in range(1, rows):
                        grad = grad + dkv_recv[b, part, cut].astype(jnp.float32)
                    final[1 + part, cut] = grad.astype(jnp.bfloat16)
                    give_back(1 + part, p)

    for which in range(3):
        for k in range(1, n_out):
            arrival(which, k).wait_send()
    for a in range(1, columns):
        gather(2, a, 0).wait_send()

    ordered(finish_queries, finish_keys)

    for n in range(n_out + 1):
        for a in range(1, columns):
            total(0, a, n).wait_send()
        for b in range(1, rows):
            total(1, b, n).wait_send()
    for which in range(3):
        text_copy(which).wait()
        out_copy(which, 0).wait()
        others = images[which].at[:, pl.ds(0, (n_out - 1) * d)]
        sent = final.at[which, pl.ds(0, (n_out - 1) * tokens)]
        pltpu.make_async_copy(sent, sent, out_send.at[which]).wait()
        pltpu.make_async_copy(others, others, out_recv.at[which]).wait()


def tail(*refs):
    sources, targets, held = refs[:6], refs[6:12], refs[12:18]
    sem = refs[18]
    loads = [pltpu.make_async_copy(s, h, sem.at[0, n]) for n, (s, h) in enumerate(zip(sources, held))]
    stores = [pltpu.make_async_copy(h, t, sem.at[1, n]) for n, (h, t) in enumerate(zip(held, targets))]
    for load in loads:
        load.start()
    for load, store in zip(loads, stores):
        load.wait()
        store.start()
    for store in stores:
        store.wait()


def shards(
    mesh,
    query_image,
    key_image,
    value_image,
    attended_image,
    upstream_image,
    logsum_image,
    query_text,
    key_text,
    value_text,
    attended_text,
    upstream_text,
    logsum_text,
):
    n_out, n_in = mesh.shape["outer"], mesh.shape["inner"]
    rows = max(c for c in range(1, math.isqrt(n_in) + 1) if n_in % c == 0)
    columns = n_in // rows
    tokens, width = query_image.shape
    block = tokens * n_out
    share = query_text.shape[0] // n_in
    span = block + share
    d = HEAD_DIM
    text_lines = logsum_text.reshape(n_in, 1, share)
    half, full = jnp.bfloat16, jnp.float32
    dma = pltpu.SemaphoreType.DMA
    vmem = pl.BlockSpec(memory_space=pltpu.VMEM)
    hbm = pl.BlockSpec(memory_space=pl.ANY)
    image_out = jax.ShapeDtypeStruct((tokens, width), half)
    text_out = jax.ShapeDtypeStruct((share, d), half)
    grads = pl.pallas_call(
        functools.partial(kernel, (n_out, n_in, rows, columns, tokens, block, share)),
        out_shape=(image_out,) * 3 + (text_out,) * 3,
        in_specs=[hbm] * 5 + [vmem] + [hbm] * 5 + [vmem],
        out_specs=(hbm,) * 6,
        scratch_shapes=[
            pltpu.VMEM((columns, 2, span, d), half),
            pltpu.VMEM((rows, 2, span, d), half),
            pltpu.VMEM((rows, d, span), half),
            pltpu.VMEM((n_out, LANES), full),
            pltpu.VMEM((n_out, 2, LANES), full),
            pltpu.VMEM((columns, n_out, 2, LANES), full),
            pltpu.VMEM((columns, 2, span), full),
            pltpu.VMEM((tokens, width), half),
            pltpu.VMEM((2, 2, tokens, width), half),
            pltpu.VMEM((columns, share, d), half),
            pltpu.VMEM((columns, d, span), full),
            pltpu.VMEM((rows, 2, span, d), full),
            pltpu.VMEM((span, d), full),
            pltpu.VMEM((columns, span, d), half),
            pltpu.VMEM((columns, span, d), half),
            pltpu.VMEM((rows, 2, span, d), half),
            pltpu.VMEM((rows, 2, span, d), half),
            pltpu.VMEM((3, span, d), half),
            dma((5,)),
            dma((2 * rows + 3 * columns,)),
            dma((3, n_out)),
            dma((3, n_out)),
            dma((3, max(rows, columns), n_out)),
            dma((3, max(rows, columns), n_out)),
            dma((2, max(rows, columns), n_out + 1)),
            dma((2, max(rows, columns), n_out + 1)),
            dma((3,)),
            dma((3,)),
            dma((2, 3)),
        ],
        compiler_params=pltpu.CompilerParams(collective_id=0, has_side_effects=True),
    )(
        query_image, key_image, value_image, attended_image, upstream_image, logsum_image.T,
        query_text, key_text, value_text, attended_text, upstream_text, text_lines,
    )
    return pl.pallas_call(
        tail,
        out_shape=(image_out,) * 3 + (text_out,) * 3,
        in_specs=[hbm] * 6,
        out_specs=(hbm,) * 6,
        scratch_shapes=[pltpu.VMEM((tokens, width), half)] * 3
        + [pltpu.VMEM((share, d), half)] * 3
        + [dma((2, 6))],
    )(*grads)


def solution(mesh):
    tokens_spec = P(("outer", "inner"), None)
    return jax.shard_map(
        functools.partial(shards, mesh),
        mesh=mesh,
        in_specs=(tokens_spec,) * 6 + (P(None, "outer"),) * 6,
        out_specs=(tokens_spec,) * 3 + (P("inner", "outer"),) * 3,
        check_vma=False,
    )
```

```python
import functools
import math

import jax
import jax.numpy as jnp
from jax import lax
from jax.experimental import pallas as pl
from jax.experimental.pallas import tpu as pltpu
from jax.sharding import PartitionSpec as P

HEAD_DIM = 128
LANES = 128
LOG2E = math.log2(math.e)
MESH = pl.DeviceIdType.MESH


def across_rows(left, right, **options):
    return lax.dot_general(
        left, right, (((1,), (1,)), ((), ())), preferred_element_type=jnp.float32, **options
    )


def ring_steps(n_out):
    cores = 2 if n_out % 2 == 0 else 1
    chips = 2 if n_out // cores % 2 == 0 else 1
    steps = [
        (far, chip, core)
        for far in range(n_out // (cores * chips))
        for chip in range(chips)
        for core in range(cores)
    ]
    return cores, chips, sorted(steps, key=lambda s: ((s[0] > 0) + (s[1] > 0), s[2] if s[0] + s[1] else 0, s))


def kernel(
    dims,
    q_ref, k_ref, v_ref, o_ref, g_ref, l_ref,
    qt_ref, kt_ref, vt_ref, ot_ref, gt_ref, lt_ref,
    out_q, out_k, out_v, out_qt, out_kt, out_vt,
    qg, kv, key_flip, lines_in, stat_send, stat, row_stat, own_o, own_l, staged, text_o, text_l,
    dq_acc, dkv_acc, dq_own, dq_send, dq_recv, dkv_send, dkv_recv, final,
    local_sem, text_sem, in_send, in_recv, gather_send, gather_recv,
    sum_send, sum_recv, out_send, out_recv, out_local,
):
    n_out, n_in, rows, columns, tokens, block, share = dims
    span = block + share
    d = HEAD_DIM
    scale = HEAD_DIM ** (-0.5)
    o = lax.axis_index("outer")
    i = lax.axis_index("inner")

    line, place_in = i // rows, i % rows

    def row_peer(a):
        return (line + a) % columns * rows + place_in

    def column_peer(b):
        return line * rows + (place_in + b) % rows

    cores, chips, steps = ring_steps(n_out)
    core, chip, far = o % cores, o // cores % chips, o // (cores * chips)

    def stepped(k, sign):
        far_step, chip_step, core_step = steps[k]
        groups = n_out // (cores * chips)
        there = (far + sign * far_step + groups) % groups * chips
        there = (there + (chip + sign * chip_step + chips) % chips) * cores
        return there + (core + sign * core_step + cores) % cores

    def other(k):
        return stepped(k, 1)

    own_loads = [
        pltpu.make_async_copy(k_ref, staged.at[0, 0], local_sem.at[0]),
        pltpu.make_async_copy(v_ref, staged.at[0, 1], local_sem.at[1]),
        pltpu.make_async_copy(q_ref, staged.at[1, 0], local_sem.at[2]),
        pltpu.make_async_copy(g_ref, staged.at[1, 1], local_sem.at[3]),
        pltpu.make_async_copy(o_ref, own_o, local_sem.at[4]),
        pltpu.make_async_copy(l_ref, own_l, local_sem.at[5]),
    ]
    for copy in own_loads:
        copy.start()

    barrier = pltpu.get_barrier_semaphore()
    for k in range(1, n_out):
        pl.semaphore_signal(barrier, inc=1, device_id=(other(k), i), device_id_type=MESH)
    for k in range(cores):
        for a in range(1, columns):
            pl.semaphore_signal(barrier, inc=1, device_id=(other(k), row_peer(a)), device_id_type=MESH)
        for b in range(1, rows):
            pl.semaphore_signal(barrier, inc=1, device_id=(other(k), column_peer(b)), device_id_type=MESH)

    text_loads = []

    def text_load(source, target):
        copy = pltpu.make_async_copy(source, target, text_sem.at[len(text_loads)])
        copy.start()
        text_loads.append(copy)

    def share_of(ref, peer):
        return ref.at[pl.ds(pl.multiple_of(peer * share, share), share)]

    text = pl.ds(block, share)
    for b in range(rows):
        text_load(share_of(kt_ref, column_peer(b)), kv.at[b, 0, text])
        text_load(share_of(vt_ref, column_peer(b)), kv.at[b, 1, text])
    for a in range(columns):
        text_load(share_of(qt_ref, row_peer(a)), qg.at[a, 0, text])
        text_load(share_of(gt_ref, row_peer(a)), qg.at[a, 1, text])
        text_load(share_of(ot_ref, row_peer(a)), text_o.at[a])
        text_load(lt_ref.at[row_peer(a)], text_l.at[a])

    pl.semaphore_wait(barrier, n_out - 1 + cores * (columns - 1 + rows - 1))

    def piece(k):
        return pl.ds(k * tokens, tokens)

    def exchange(which, source, target, k):
        if k == 0:
            return pltpu.make_async_copy(source, target, in_recv.at[which, 0])
        return pltpu.make_async_remote_copy(
            src_ref=source,
            dst_ref=target,
            send_sem=in_send.at[which, k],
            recv_sem=in_recv.at[which, k],
            device_id=(other(k), i),
            device_id_type=MESH,
        )

    def head_of(which, k):
        return staged.at[which, :, :, pl.ds(pl.multiple_of(other(k) * d, d), d)]

    homes = (kv, qg)
    sizes = (rows, columns, columns)

    def arrival(which, k):
        if which == 2:
            return exchange(2, stat_send.at[other(k)], stat.at[0, k], k)
        return exchange(which, head_of(which, k), homes[which].at[0, :, piece(k)], k)

    def gather(which, offset, k):
        place = (sizes[which] - offset) % sizes[which]
        if which == 2:
            source, target = stat.at[0], stat.at[place]
        else:
            source = head_of(which, k) if k < cores else homes[which].at[0, :, piece(k)]
            target = homes[which].at[place, :, piece(k)]
        peer = row_peer(offset) if which else column_peer(offset)
        return pltpu.make_async_remote_copy(
            src_ref=source,
            dst_ref=target,
            send_sem=gather_send.at[which, offset, k],
            recv_sem=gather_recv.at[which, place, k],
            device_id=(other(k) if which < 2 and k < cores else o, peer),
            device_id_type=MESH,
        )

    at_end = jnp.logical_or(i == 0, i == n_in - 1)

    def ordered(first, second):
        @pl.when(at_end)
        def _():
            first()
            second()

        @pl.when(jnp.logical_not(at_end))
        def _():
            second()
            first()

    def depart(which):
        for k in range(cores):
            for offset in range(1, sizes[which]):
                gather(which, offset, k).start()
        for k in (*range(cores, n_out), *range(cores)):
            arrival(which, k).start()

    for copy in own_loads:
        copy.wait()
    ordered(lambda: depart(0), lambda: depart(1))

    lane = lax.broadcasted_iota(jnp.int32, (1, LANES), 1)
    ones = jnp.ones((8, d), jnp.float32)
    repeats = LANES // tokens
    lines_in[...] = jnp.zeros_like(lines_in)
    lines_in[:, 0:tokens] = own_l[...]
    image_lines = lines_in[...]
    for p in range(1, repeats):
        moved = pltpu.roll(lines_in[...], p * tokens, 1)
        image_lines = jnp.where(lane // tokens == p, moved, image_lines)
    image_lines = image_lines * LOG2E
    for h in range(n_out):
        cut = slice(h * d, (h + 1) * d)
        product = staged[1, 1, :, cut].astype(jnp.float32) * own_o[:, cut].astype(jnp.float32)
        product = jnp.concatenate([product] * repeats, axis=0)
        delta = across_rows(ones, product, precision=lax.Precision.HIGHEST)
        stat_send[h, 0:1, :] = image_lines[h : h + 1, :]
        stat_send[h, 1:2, :] = delta[0:1, :]
    for k in range(n_out):
        arrival(2, k).start()

    def landed(which, k):
        if k == 0:
            arrival(which, k).wait()
        else:
            arrival(which, k).wait_recv()

    def forward(which):
        for k in range(cores, n_out):
            landed(which, k)
            for offset in range(1, sizes[which]):
                gather(which, offset, k).start()

    ordered(lambda: forward(0), lambda: forward(1))
    for which in range(2):
        for k in range(cores):
            landed(which, k)
    for k in range(n_out):
        landed(2, k)
    for offset in range(1, columns):
        gather(2, offset, 0).start()

    for copy in text_loads:
        copy.wait()
    for a in range(columns):
        product = qg[a, 1, text].astype(jnp.float32) * text_o[a].astype(jnp.float32)
        delta = across_rows(ones, product, precision=lax.Precision.HIGHEST)
        row_stat[a, 0:1, text] = text_l[a] * LOG2E
        row_stat[a, 1:2, text] = delta[0:1, :]

    dq_acc[...] = jnp.zeros_like(dq_acc)
    dkv_acc[...] = jnp.zeros_like(dkv_acc)

    def spread_statistics(a):
        for start in range(0, block, LANES):
            first = start // tokens
            lines = [stat[a, first + p] for p in range(min(repeats, n_out - first))]
            merged = lines[0]
            for p in range(1, len(lines)):
                merged = jnp.where(lane // tokens == p, lines[p], merged)
            row_stat[a, :, start : start + LANES] = merged

    def flip_keys(b):
        key_flip[b] = kv[b, 0].astype(jnp.float32).T.astype(jnp.bfloat16)

    size = math.gcd(block, 256)
    chunks = [(start, size) for start in range(0, block, size)] + [(block, share)]

    def total(kind, offset, n):
        group = rows if kind else columns
        place = (group - offset) % group
        cut = piece(n) if n < n_out else text
        if kind:
            source, target = dkv_send.at[offset, :, cut], dkv_recv.at[place, :, cut]
        else:
            source, target = dq_send.at[offset, cut], dq_recv.at[place, cut]
        peer = column_peer(offset) if kind else row_peer(offset)
        return pltpu.make_async_remote_copy(
            src_ref=source,
            dst_ref=target,
            send_sem=sum_send.at[kind, offset, n],
            recv_sem=sum_recv.at[kind, place, n],
            device_id=(o, peer),
            device_id_type=MESH,
        )

    def pieces(n):
        start, length = chunks[n]
        return range(start // tokens, (start + length) // tokens) if start < block else (n_out,)

    def query_sum(a, n):
        start, length = chunks[n]
        return dq_acc[a, :, start : start + length].T * scale

    def work(a, b, n):
        start, length = chunks[n]
        cut = slice(start, start + length)
        keys, values = kv[b, 0], kv[b, 1]
        queries, upstream = qg[a, 0, cut], qg[a, 1, cut]
        scores = across_rows(keys, queries) * (scale * LOG2E)
        weights = jnp.exp2(scores - row_stat[a, 0:1, cut])
        slopes = across_rows(values, upstream)
        mixed = (weights * (slopes - row_stat[a, 1:2, cut])).astype(jnp.bfloat16)
        weights = weights.astype(jnp.bfloat16)
        dkv_acc[b, 1] += jnp.dot(weights, upstream, preferred_element_type=jnp.float32)
        dkv_acc[b, 0] += jnp.dot(mixed, queries, preferred_element_type=jnp.float32)
        dq_acc[a, :, cut] += jnp.dot(key_flip[b], mixed, preferred_element_type=jnp.float32)

    def work_keys(a, b, n):
        start, length = chunks[n]
        cut = slice(start, start + length)
        keys, values = kv[b, 0, cut], kv[b, 1, cut]
        queries, upstream = qg[a, 0], qg[a, 1]
        scores = across_rows(keys, queries) * (scale * LOG2E)
        weights = jnp.exp2(scores - row_stat[a, 0:1])
        slopes = across_rows(values, upstream)
        mixed = (weights * (slopes - row_stat[a, 1:2])).astype(jnp.bfloat16)
        weights = weights.astype(jnp.bfloat16)
        dkv_acc[b, 1, cut] += jnp.dot(weights, upstream, preferred_element_type=jnp.float32)
        dkv_acc[b, 0, cut] += jnp.dot(mixed, queries, preferred_element_type=jnp.float32)
        dq_acc[a] += jnp.dot(key_flip[b, :, cut], mixed, preferred_element_type=jnp.float32)

    spread_statistics(0)
    flip_keys(0)
    for n in range(len(chunks)):
        work(0, 0, n)

    def near_keys_landed(b, n):
        start, length = chunks[n]
        if start < block:
            for k in range(start // tokens, (start + length) // tokens):
                gather(0, (rows - b) % rows, k).wait_recv()
        cut = slice(start, start + length)
        key_flip[b, :, cut] = kv[b, 0, cut].astype(jnp.float32).T.astype(jnp.bfloat16)

    def far_queries_landed(a, n):
        start, length = chunks[n]
        if start < block:
            for k in range(start // tokens, (start + length) // tokens):
                gather(1, (columns - a) % columns, k).wait_recv()
        if start == 0:
            gather(2, (columns - a) % columns, 0).wait_recv()
            spread_statistics(a)

    def gathers_left(which):
        for offset in range(1, sizes[which]):
            for k in range(n_out):
                gather(which, offset, k).wait_send()

    def send_queries(a, n, order=iter):
        start, length = chunks[n]
        dq_send[a, start : start + length] = query_sum(a, n).astype(jnp.bfloat16)
        for p in order(pieces(n)):
            total(0, a, p).start()

    def send_keys(b, n, order=iter):
        start, length = chunks[n]
        cut = slice(start, start + length)
        dkv_send[b, 0, cut] = (dkv_acc[b, 0, cut] * scale).astype(jnp.bfloat16)
        dkv_send[b, 1, cut] = dkv_acc[b, 1, cut].astype(jnp.bfloat16)
        for p in order(pieces(n)):
            total(1, b, p).start()

    places = (len(chunks) - 1, *range(len(chunks) - 1))
    outward = (*reversed(range(len(chunks) - 1)), len(chunks) - 1)

    def loop(first, last, body):
        def with_carry(index, carry):
            body(index)
            return carry

        if last - first <= 2:
            for index in range(first, last):
                body(index)
        else:
            lax.fori_loop(first, last, with_carry, 0)

    @pl.when(jnp.logical_not(at_end))
    def _():
        def near_keys(b):
            for n in places:
                near_keys_landed(b, n)
            for n in places:
                work(0, b, n)

        def far_queries(a):
            for n in places[:-1]:
                far_queries_landed(a, n)
                loop(0, rows, lambda b: work(a, rows - 1 - b, n))
                send_queries(a, n)

        def give_keys(b):
            for n in outward:
                send_keys(b, n, reversed)

        def last_queries(a):
            n = places[-1]
            far_queries_landed(a, n)
            loop(1, rows, lambda b: work(a, b, n))

        def give_queries(a):
            work(a, 0, places[-1])
            send_queries(a, places[-1])

        loop(1, rows, near_keys)
        loop(1, columns, far_queries)
        loop(1, columns, last_queries)
        loop(1, rows, give_keys)
        loop(1, columns, give_queries)
        gathers_left(0)
        gathers_left(1)

    @pl.when(at_end)
    def _():
        def far_queries(a):
            for n in places:
                far_queries_landed(a, n)
                work(a, 0, n)

        def near_keys(b):
            for n in places:
                near_keys_landed(b, n)
                loop(0, columns, lambda a: work_keys(a, b, n))
                send_keys(b, n)

        def give_queries(a):
            for n in outward:
                send_queries(a, n, reversed)

        loop(1, columns, far_queries)
        loop(1, rows, near_keys)
        loop(1, columns, give_queries)
        gathers_left(0)
        gathers_left(1)

    mine = pl.ds(pl.multiple_of(o * d, d), d)
    images, texts = (out_q, out_k, out_v), (out_qt, out_kt, out_vt)

    def out_copy(which, k):
        source, target = final.at[which, piece(k)], images[which].at[:, mine]
        if k == 0:
            return pltpu.make_async_copy(source, target, out_local.at[0, which])
        return pltpu.make_async_remote_copy(
            src_ref=source,
            dst_ref=target,
            send_sem=out_send.at[which],
            recv_sem=out_recv.at[which],
            device_id=(stepped(k, -1), i),
            device_id_type=MESH,
        )

    def text_copy(which):
        return pltpu.make_async_copy(final.at[which, text], texts[which], out_local.at[1, which])

    def give_back(which, p):
        if p < n_out:
            out_copy(which, p).start()
        else:
            text_copy(which).start()

    def finish_queries(places, order):
        for n in range(len(chunks)):
            start, length = chunks[n]
            dq_own[start : start + length] = query_sum(0, n)
        for n in places:
            for p in order(pieces(n)):
                cut = piece(p) if p < n_out else text
                grad = dq_own[cut]
                for a in range(1, columns):
                    total(0, (columns - a) % columns, p).wait_recv()
                    grad = grad + dq_recv[a, cut].astype(jnp.float32)
                final[0, cut] = grad.astype(jnp.bfloat16)
                give_back(0, p)

    def finish_keys(places, order):
        for n in places:
            for p in order(pieces(n)):
                cut = piece(p) if p < n_out else text
                for b in range(1, rows):
                    total(1, (rows - b) % rows, p).wait_recv()
                for part in (0, 1):
                    grad = dkv_acc[0, part, cut]
                    if part == 0:
                        grad = grad * scale
                    for b in range(1, rows):
                        grad = grad + dkv_recv[b, part, cut].astype(jnp.float32)
                    final[1 + part, cut] = grad.astype(jnp.bfloat16)
                    give_back(1 + part, p)

    for which in range(3):
        for k in range(1, n_out):
            arrival(which, k).wait_send()
    for a in range(1, columns):
        gather(2, a, 0).wait_send()

    @pl.when(at_end)
    def _():
        finish_queries(places, iter)
        finish_keys(outward, reversed)

    @pl.when(jnp.logical_not(at_end))
    def _():
        finish_keys(places, iter)
        finish_queries(outward, reversed)


    for n in range(n_out + 1):
        for a in range(1, columns):
            total(0, a, n).wait_send()
        for b in range(1, rows):
            total(1, b, n).wait_send()
    for which in range(3):
        text_copy(which).wait()
        out_copy(which, 0).wait()
        others = images[which].at[:, pl.ds(0, (n_out - 1) * d)]
        sent = final.at[which, pl.ds(0, (n_out - 1) * tokens)]
        pltpu.make_async_copy(sent, sent, out_send.at[which]).wait()
        pltpu.make_async_copy(others, others, out_recv.at[which]).wait()


def tail(*refs):
    sources, targets, held = refs[:6], refs[6:12], refs[12:18]
    sem = refs[18]
    loads = [pltpu.make_async_copy(s, h, sem.at[0, n]) for n, (s, h) in enumerate(zip(sources, held))]
    stores = [pltpu.make_async_copy(h, t, sem.at[1, n]) for n, (h, t) in enumerate(zip(held, targets))]
    for load in loads:
        load.start()
    for load, store in zip(loads, stores):
        load.wait()
        store.start()
    for store in stores:
        store.wait()


def shards(
    mesh,
    query_image,
    key_image,
    value_image,
    attended_image,
    upstream_image,
    logsum_image,
    query_text,
    key_text,
    value_text,
    attended_text,
    upstream_text,
    logsum_text,
):
    n_out, n_in = mesh.shape["outer"], mesh.shape["inner"]
    rows = max(c for c in range(1, math.isqrt(n_in) + 1) if n_in % c == 0)
    columns = n_in // rows
    tokens, width = query_image.shape
    block = tokens * n_out
    share = query_text.shape[0] // n_in
    span = block + share
    d = HEAD_DIM
    text_lines = logsum_text.reshape(n_in, 1, share)
    half, full = jnp.bfloat16, jnp.float32
    dma = pltpu.SemaphoreType.DMA
    hbm = pl.BlockSpec(memory_space=pl.ANY)
    image_out = jax.ShapeDtypeStruct((tokens, width), half)
    text_out = jax.ShapeDtypeStruct((share, d), half)
    grads = pl.pallas_call(
        functools.partial(kernel, (n_out, n_in, rows, columns, tokens, block, share)),
        out_shape=(image_out,) * 3 + (text_out,) * 3,
        in_specs=[hbm] * 12,
        out_specs=(hbm,) * 6,
        scratch_shapes=[
            pltpu.VMEM((columns, 2, span, d), half),
            pltpu.VMEM((rows, 2, span, d), half),
            pltpu.VMEM((rows, d, span), half),
            pltpu.VMEM((n_out, LANES), full),
            pltpu.VMEM((n_out, 2, LANES), full),
            pltpu.VMEM((columns, n_out, 2, LANES), full),
            pltpu.VMEM((columns, 2, span), full),
            pltpu.VMEM((tokens, width), half),
            pltpu.VMEM((n_out, tokens), full),
            pltpu.VMEM((2, 2, tokens, width), half),
            pltpu.VMEM((columns, share, d), half),
            pltpu.VMEM((columns, 1, share), full),
            pltpu.VMEM((columns, d, span), full),
            pltpu.VMEM((rows, 2, span, d), full),
            pltpu.VMEM((span, d), full),
            pltpu.VMEM((columns, span, d), half),
            pltpu.VMEM((columns, span, d), half),
            pltpu.VMEM((rows, 2, span, d), half),
            pltpu.VMEM((rows, 2, span, d), half),
            pltpu.VMEM((3, span, d), half),
            dma((6,)),
            dma((2 * rows + 4 * columns,)),
            dma((3, n_out)),
            dma((3, n_out)),
            dma((3, max(rows, columns), n_out)),
            dma((3, max(rows, columns), n_out)),
            dma((2, max(rows, columns), n_out + 1)),
            dma((2, max(rows, columns), n_out + 1)),
            dma((3,)),
            dma((3,)),
            dma((2, 3)),
        ],
        compiler_params=pltpu.CompilerParams(collective_id=0, has_side_effects=True),
    )(
        query_image, key_image, value_image, attended_image, upstream_image, logsum_image.T,
        query_text, key_text, value_text, attended_text, upstream_text, text_lines,
    )
    return pl.pallas_call(
        tail,
        out_shape=(image_out,) * 3 + (text_out,) * 3,
        in_specs=[hbm] * 6,
        out_specs=(hbm,) * 6,
        scratch_shapes=[pltpu.VMEM((tokens, width), half)] * 3
        + [pltpu.VMEM((share, d), half)] * 3
        + [dma((2, 6))],
    )(*grads)


def solution(mesh):
    tokens_spec = P(("outer", "inner"), None)
    return jax.shard_map(
        functools.partial(shards, mesh),
        mesh=mesh,
        in_specs=(tokens_spec,) * 6 + (P(None, "outer"),) * 6,
        out_specs=(tokens_spec,) * 3 + (P("inner", "outer"),) * 3,
        check_vma=False,
    )
```

```python
import functools
import math

import jax
import jax.numpy as jnp
from jax import lax
from jax.experimental import pallas as pl
from jax.experimental.pallas import tpu as pltpu
from jax.sharding import PartitionSpec as P

HEAD_DIM = 128
LANES = 128
LOG2E = math.log2(math.e)
MESH = pl.DeviceIdType.MESH


def across_rows(left, right, **options):
    return lax.dot_general(
        left, right, (((1,), (1,)), ((), ())), preferred_element_type=jnp.float32, **options
    )


def ring_steps(n_out):
    cores = 2 if n_out % 2 == 0 else 1
    chips = 2 if n_out // cores % 2 == 0 else 1
    steps = [
        (far, chip, core)
        for far in range(n_out // (cores * chips))
        for chip in range(chips)
        for core in range(cores)
    ]
    return cores, chips, sorted(steps, key=lambda s: ((s[0] > 0) + (s[1] > 0), s[2] if s[0] + s[1] else 0, s))


def kernel(
    dims,
    q_ref, k_ref, v_ref, o_ref, g_ref, l_ref,
    qt_ref, kt_ref, vt_ref, ot_ref, gt_ref, lt_ref,
    out_q, out_k, out_v, out_qt, out_kt, out_vt,
    qg, kv, key_flip, lines_in, stat_send, stat, row_stat, own_o, own_l, staged, text_o, text_l,
    dq_acc, dkv_acc, dq_own, dq_send, dq_recv, dkv_send, dkv_recv, final,
    local_sem, text_sem, in_send, in_recv, gather_send, gather_recv,
    sum_send, sum_recv, out_send, out_recv, out_local,
):
    n_out, n_in, rows, columns, tokens, block, share = dims
    span = block + share
    d = HEAD_DIM
    scale = HEAD_DIM ** (-0.5)
    o = lax.axis_index("outer")
    i = lax.axis_index("inner")

    line, place_in = i // rows, i % rows

    def row_peer(a):
        return (line + a) % columns * rows + place_in

    def column_peer(b):
        return line * rows + (place_in + b) % rows

    cores, chips, steps = ring_steps(n_out)
    core, chip, far = o % cores, o // cores % chips, o // (cores * chips)

    def stepped(k, sign):
        far_step, chip_step, core_step = steps[k]
        groups = n_out // (cores * chips)
        there = (far + sign * far_step + groups) % groups * chips
        there = (there + (chip + sign * chip_step + chips) % chips) * cores
        return there + (core + sign * core_step + cores) % cores

    def other(k):
        return stepped(k, 1)

    own_loads = [
        pltpu.make_async_copy(k_ref, staged.at[0, 0], local_sem.at[0]),
        pltpu.make_async_copy(v_ref, staged.at[0, 1], local_sem.at[1]),
        pltpu.make_async_copy(q_ref, staged.at[1, 0], local_sem.at[2]),
        pltpu.make_async_copy(g_ref, staged.at[1, 1], local_sem.at[3]),
        pltpu.make_async_copy(o_ref, own_o, local_sem.at[4]),
        pltpu.make_async_copy(l_ref, own_l, local_sem.at[5]),
    ]
    for copy in own_loads:
        copy.start()

    barrier = pltpu.get_barrier_semaphore()
    for k in range(1, n_out):
        pl.semaphore_signal(barrier, inc=1, device_id=(other(k), i), device_id_type=MESH)
    for k in range(cores):
        for a in range(1, columns):
            pl.semaphore_signal(barrier, inc=1, device_id=(other(k), row_peer(a)), device_id_type=MESH)
        for b in range(1, rows):
            pl.semaphore_signal(barrier, inc=1, device_id=(other(k), column_peer(b)), device_id_type=MESH)

    text_loads = []

    def text_load(source, target):
        copy = pltpu.make_async_copy(source, target, text_sem.at[len(text_loads)])
        copy.start()
        text_loads.append(copy)

    def share_of(ref, peer):
        return ref.at[pl.ds(pl.multiple_of(peer * share, share), share)]

    text = pl.ds(block, share)
    for b in range(rows):
        text_load(share_of(kt_ref, column_peer(b)), kv.at[b, 0, text])
        text_load(share_of(vt_ref, column_peer(b)), kv.at[b, 1, text])
    for a in range(columns):
        text_load(share_of(qt_ref, row_peer(a)), qg.at[a, 0, text])
        text_load(share_of(gt_ref, row_peer(a)), qg.at[a, 1, text])
        text_load(share_of(ot_ref, row_peer(a)), text_o.at[a])
        text_load(lt_ref.at[row_peer(a)], text_l.at[a])

    pl.semaphore_wait(barrier, n_out - 1 + cores * (columns - 1 + rows - 1))

    def piece(k):
        return pl.ds(k * tokens, tokens)

    def exchange(which, source, target, k):
        if k == 0:
            return pltpu.make_async_copy(source, target, in_recv.at[which, 0])
        return pltpu.make_async_remote_copy(
            src_ref=source,
            dst_ref=target,
            send_sem=in_send.at[which, k],
            recv_sem=in_recv.at[which, k],
            device_id=(other(k), i),
            device_id_type=MESH,
        )

    def head_of(which, k):
        return staged.at[which, :, :, pl.ds(pl.multiple_of(other(k) * d, d), d)]

    homes = (kv, qg)
    sizes = (rows, columns, columns)

    def arrival(which, k):
        if which == 2:
            return exchange(2, stat_send.at[other(k)], stat.at[0, k], k)
        return exchange(which, head_of(which, k), homes[which].at[0, :, piece(k)], k)

    def gather(which, offset, k):
        place = (sizes[which] - offset) % sizes[which]
        if which == 2:
            source, target = stat.at[0], stat.at[place]
        else:
            source = head_of(which, k) if k < cores else homes[which].at[0, :, piece(k)]
            target = homes[which].at[place, :, piece(k)]
        peer = row_peer(offset) if which else column_peer(offset)
        return pltpu.make_async_remote_copy(
            src_ref=source,
            dst_ref=target,
            send_sem=gather_send.at[which, offset, k],
            recv_sem=gather_recv.at[which, place, k],
            device_id=(other(k) if which < 2 and k < cores else o, peer),
            device_id_type=MESH,
        )

    at_end = jnp.logical_or(i == 0, i == n_in - 1)

    def ordered(first, second):
        @pl.when(at_end)
        def _():
            first()
            second()

        @pl.when(jnp.logical_not(at_end))
        def _():
            second()
            first()

    def depart(which):
        for k in range(cores):
            for offset in range(1, sizes[which]):
                gather(which, offset, k).start()
        for k in (*range(cores, n_out), *range(cores)):
            arrival(which, k).start()

    for copy in own_loads:
        copy.wait()
    ordered(lambda: depart(0), lambda: depart(1))

    lane = lax.broadcasted_iota(jnp.int32, (1, LANES), 1)
    ones = jnp.ones((8, d), jnp.float32)
    repeats = LANES // tokens
    lines_in[...] = jnp.zeros_like(lines_in)
    lines_in[:, 0:tokens] = own_l[...]
    image_lines = lines_in[...]
    for p in range(1, repeats):
        moved = pltpu.roll(lines_in[...], p * tokens, 1)
        image_lines = jnp.where(lane // tokens == p, moved, image_lines)
    image_lines = image_lines * LOG2E
    for h in range(n_out):
        cut = slice(h * d, (h + 1) * d)
        product = staged[1, 1, :, cut].astype(jnp.float32) * own_o[:, cut].astype(jnp.float32)
        product = jnp.concatenate([product] * repeats, axis=0)
        delta = across_rows(ones, product, precision=lax.Precision.HIGHEST)
        stat_send[h, 0:1, :] = image_lines[h : h + 1, :]
        stat_send[h, 1:2, :] = delta[0:1, :]
    for k in range(n_out):
        arrival(2, k).start()

    def landed(which, k):
        if k == 0:
            arrival(which, k).wait()
        else:
            arrival(which, k).wait_recv()

    def forward(which):
        for k in range(cores, n_out):
            landed(which, k)
            for offset in range(1, sizes[which]):
                gather(which, offset, k).start()

    ordered(lambda: forward(0), lambda: forward(1))
    for which in range(2):
        for k in range(cores):
            landed(which, k)
    for k in range(n_out):
        landed(2, k)
    for offset in range(1, columns):
        gather(2, offset, 0).start()

    for copy in text_loads:
        copy.wait()
    for a in range(columns):
        product = qg[a, 1, text].astype(jnp.float32) * text_o[a].astype(jnp.float32)
        delta = across_rows(ones, product, precision=lax.Precision.HIGHEST)
        row_stat[a, 0:1, text] = text_l[a] * LOG2E
        row_stat[a, 1:2, text] = delta[0:1, :]

    dq_acc[...] = jnp.zeros_like(dq_acc)
    dkv_acc[...] = jnp.zeros_like(dkv_acc)

    def spread_statistics(a):
        for start in range(0, block, LANES):
            first = start // tokens
            lines = [stat[a, first + p] for p in range(min(repeats, n_out - first))]
            merged = lines[0]
            for p in range(1, len(lines)):
                merged = jnp.where(lane // tokens == p, lines[p], merged)
            row_stat[a, :, start : start + LANES] = merged

    def flip_keys(b):
        key_flip[b] = kv[b, 0].astype(jnp.float32).T.astype(jnp.bfloat16)

    size = math.gcd(block, 256)
    chunks = [(start, size) for start in range(0, block, size)] + [(block, share)]

    def total(kind, offset, n):
        group = rows if kind else columns
        place = (group - offset) % group
        cut = piece(n) if n < n_out else text
        if kind:
            source, target = dkv_send.at[offset, :, cut], dkv_recv.at[place, :, cut]
        else:
            source, target = dq_send.at[offset, cut], dq_recv.at[place, cut]
        peer = column_peer(offset) if kind else row_peer(offset)
        return pltpu.make_async_remote_copy(
            src_ref=source,
            dst_ref=target,
            send_sem=sum_send.at[kind, offset, n],
            recv_sem=sum_recv.at[kind, place, n],
            device_id=(o, peer),
            device_id_type=MESH,
        )

    def pieces(n):
        start, length = chunks[n]
        return range(start // tokens, (start + length) // tokens) if start < block else (n_out,)

    def query_sum(a, n):
        start, length = chunks[n]
        return dq_acc[a, :, start : start + length].T * scale

    def work(a, b, n):
        start, length = chunks[n]
        cut = slice(start, start + length)
        keys, values = kv[b, 0], kv[b, 1]
        queries, upstream = qg[a, 0, cut], qg[a, 1, cut]
        scores = across_rows(keys, queries) * (scale * LOG2E)
        weights = jnp.exp2(scores - row_stat[a, 0:1, cut])
        slopes = across_rows(values, upstream)
        mixed = (weights * (slopes - row_stat[a, 1:2, cut])).astype(jnp.bfloat16)
        weights = weights.astype(jnp.bfloat16)
        dkv_acc[b, 1] += jnp.dot(weights, upstream, preferred_element_type=jnp.float32)
        dkv_acc[b, 0] += jnp.dot(mixed, queries, preferred_element_type=jnp.float32)
        dq_acc[a, :, cut] += jnp.dot(key_flip[b], mixed, preferred_element_type=jnp.float32)

    def work_keys(a, b, n):
        start, length = chunks[n]
        cut = slice(start, start + length)
        keys, values = kv[b, 0, cut], kv[b, 1, cut]
        queries, upstream = qg[a, 0], qg[a, 1]
        scores = across_rows(keys, queries) * (scale * LOG2E)
        weights = jnp.exp2(scores - row_stat[a, 0:1])
        slopes = across_rows(values, upstream)
        mixed = (weights * (slopes - row_stat[a, 1:2])).astype(jnp.bfloat16)
        weights = weights.astype(jnp.bfloat16)
        dkv_acc[b, 1, cut] += jnp.dot(weights, upstream, preferred_element_type=jnp.float32)
        dkv_acc[b, 0, cut] += jnp.dot(mixed, queries, preferred_element_type=jnp.float32)
        dq_acc[a] += jnp.dot(key_flip[b, :, cut], mixed, preferred_element_type=jnp.float32)

    spread_statistics(0)
    flip_keys(0)
    for n in range(len(chunks)):
        work(0, 0, n)

    def near_keys_landed(b, n):
        start, length = chunks[n]
        if start < block:
            for k in range(start // tokens, (start + length) // tokens):
                gather(0, (rows - b) % rows, k).wait_recv()
        cut = slice(start, start + length)
        key_flip[b, :, cut] = kv[b, 0, cut].astype(jnp.float32).T.astype(jnp.bfloat16)

    def far_queries_landed(a, n):
        start, length = chunks[n]
        if start < block:
            for k in range(start // tokens, (start + length) // tokens):
                gather(1, (columns - a) % columns, k).wait_recv()
        if start == 0:
            gather(2, (columns - a) % columns, 0).wait_recv()
            spread_statistics(a)

    def gathers_left(which):
        for offset in range(1, sizes[which]):
            for k in range(n_out):
                gather(which, offset, k).wait_send()

    def send_queries(a, n, order=iter):
        start, length = chunks[n]
        dq_send[a, start : start + length] = query_sum(a, n).astype(jnp.bfloat16)
        for p in order(pieces(n)):
            total(0, a, p).start()

    def send_keys(b, n, order=iter):
        start, length = chunks[n]
        cut = slice(start, start + length)
        dkv_send[b, 0, cut] = (dkv_acc[b, 0, cut] * scale).astype(jnp.bfloat16)
        dkv_send[b, 1, cut] = dkv_acc[b, 1, cut].astype(jnp.bfloat16)
        for p in order(pieces(n)):
            total(1, b, p).start()

    places = (len(chunks) - 1, *range(len(chunks) - 1))
    outward = (*reversed(range(len(chunks) - 1)), len(chunks) - 1)

    def loop(first, last, body):
        def with_carry(index, carry):
            body(index)
            return carry

        if last - first <= 2:
            for index in range(first, last):
                body(index)
        else:
            lax.fori_loop(first, last, with_carry, 0)

    @pl.when(jnp.logical_not(at_end))
    def _():
        def near_keys(b):
            for n in places:
                near_keys_landed(b, n)
            for n in places:
                work(0, b, n)

        def far_queries(a):
            for n in places[:-1]:
                far_queries_landed(a, n)
                loop(0, rows, lambda b: work(a, rows - 1 - b, n))
                send_queries(a, n)

        def give_keys(b):
            for n in outward:
                send_keys(b, n, reversed)

        def last_queries(a):
            n = places[-1]
            far_queries_landed(a, n)
            loop(1, rows, lambda b: work(a, b, n))

        def give_queries(a):
            work(a, 0, places[-1])
            send_queries(a, places[-1])

        loop(1, rows, near_keys)
        loop(1, columns, far_queries)
        loop(1, columns, last_queries)
        loop(1, rows, give_keys)
        loop(1, columns, give_queries)
        gathers_left(0)
        gathers_left(1)

    @pl.when(at_end)
    def _():
        def far_queries(a):
            for n in places:
                far_queries_landed(a, n)
                work(a, 0, n)

        def near_keys(b):
            for n in places:
                near_keys_landed(b, n)
                loop(0, columns, lambda a: work_keys(a, b, n))
                send_keys(b, n)

        def give_queries(a):
            for n in outward:
                send_queries(a, n, reversed)

        loop(1, columns, far_queries)
        loop(1, rows, near_keys)
        loop(1, columns, give_queries)
        gathers_left(0)
        gathers_left(1)

    mine = pl.ds(pl.multiple_of(o * d, d), d)
    images, texts = (out_q, out_k, out_v), (out_qt, out_kt, out_vt)

    def out_copy(which, k):
        source, target = final.at[which, piece(k)], images[which].at[:, mine]
        if k == 0:
            return pltpu.make_async_copy(source, target, out_local.at[0, which])
        return pltpu.make_async_remote_copy(
            src_ref=source,
            dst_ref=target,
            send_sem=out_send.at[which],
            recv_sem=out_recv.at[which],
            device_id=(stepped(k, -1), i),
            device_id_type=MESH,
        )

    def text_copy(which):
        return pltpu.make_async_copy(final.at[which, text], texts[which], out_local.at[1, which])

    def give_back(which, p):
        if p < n_out:
            out_copy(which, p).start()
        else:
            text_copy(which).start()

    def finish_queries(places, order):
        for n in range(len(chunks)):
            start, length = chunks[n]
            dq_own[start : start + length] = query_sum(0, n)
        for n in places:
            for p in order(pieces(n)):
                cut = piece(p) if p < n_out else text
                grad = dq_own[cut]
                for a in range(1, columns):
                    total(0, (columns - a) % columns, p).wait_recv()
                    grad = grad + dq_recv[a, cut].astype(jnp.float32)
                final[0, cut] = grad.astype(jnp.bfloat16)
                give_back(0, p)

    def finish_keys(places, order):
        for n in places:
            for p in order(pieces(n)):
                cut = piece(p) if p < n_out else text
                for b in range(1, rows):
                    total(1, (rows - b) % rows, p).wait_recv()
                for part in (0, 1):
                    grad = dkv_acc[0, part, cut]
                    if part == 0:
                        grad = grad * scale
                    for b in range(1, rows):
                        grad = grad + dkv_recv[b, part, cut].astype(jnp.float32)
                    final[1 + part, cut] = grad.astype(jnp.bfloat16)
                    give_back(1 + part, p)

    for which in range(3):
        for k in range(1, n_out):
            arrival(which, k).wait_send()
    for a in range(1, columns):
        gather(2, a, 0).wait_send()

    @pl.when(at_end)
    def _():
        finish_queries(places, iter)
        finish_keys(outward, reversed)

    @pl.when(jnp.logical_not(at_end))
    def _():
        finish_keys(places, iter)
        finish_queries(outward, reversed)


    for n in range(n_out + 1):
        for a in range(1, columns):
            total(0, a, n).wait_send()
        for b in range(1, rows):
            total(1, b, n).wait_send()
    for which in range(3):
        text_copy(which).wait()
        out_copy(which, 0).wait()
        others = images[which].at[:, pl.ds(0, (n_out - 1) * d)]
        sent = final.at[which, pl.ds(0, (n_out - 1) * tokens)]
        pltpu.make_async_copy(sent, sent, out_send.at[which]).wait()
        pltpu.make_async_copy(others, others, out_recv.at[which]).wait()


def tail(*refs):
    copies = [pltpu.make_async_copy(s, t, refs[12].at[n]) for n, (s, t) in enumerate(zip(refs[:6], refs[6:12]))]
    for copy in copies:
        copy.start()
    for copy in copies:
        copy.wait()


def shards(
    mesh,
    query_image,
    key_image,
    value_image,
    attended_image,
    upstream_image,
    logsum_image,
    query_text,
    key_text,
    value_text,
    attended_text,
    upstream_text,
    logsum_text,
):
    n_out, n_in = mesh.shape["outer"], mesh.shape["inner"]
    rows = max(c for c in range(1, math.isqrt(n_in) + 1) if n_in % c == 0)
    columns = n_in // rows
    tokens, width = query_image.shape
    block = tokens * n_out
    share = query_text.shape[0] // n_in
    span = block + share
    d = HEAD_DIM
    text_lines = logsum_text.reshape(n_in, 1, share)
    half, full = jnp.bfloat16, jnp.float32
    dma = pltpu.SemaphoreType.DMA
    hbm = pl.BlockSpec(memory_space=pl.ANY)
    image_out = jax.ShapeDtypeStruct((tokens, width), half)
    text_out = jax.ShapeDtypeStruct((share, d), half)

    def stay(array):
        return pltpu.with_memory_space_constraint(array, pltpu.HBM)

    grads = pl.pallas_call(
        functools.partial(kernel, (n_out, n_in, rows, columns, tokens, block, share)),
        out_shape=(pltpu.VMEM((tokens, width), half),) * 3 + (pltpu.VMEM((share, d), half),) * 3,
        in_specs=[hbm] * 12,
        out_specs=(hbm,) * 6,
        scratch_shapes=[
            pltpu.VMEM((columns, 2, span, d), half),
            pltpu.VMEM((rows, 2, span, d), half),
            pltpu.VMEM((rows, d, span), half),
            pltpu.VMEM((n_out, LANES), full),
            pltpu.VMEM((n_out, 2, LANES), full),
            pltpu.VMEM((columns, n_out, 2, LANES), full),
            pltpu.VMEM((columns, 2, span), full),
            pltpu.VMEM((tokens, width), half),
            pltpu.VMEM((n_out, tokens), full),
            pltpu.VMEM((2, 2, tokens, width), half),
            pltpu.VMEM((columns, share, d), half),
            pltpu.VMEM((columns, 1, share), full),
            pltpu.VMEM((columns, d, span), full),
            pltpu.VMEM((rows, 2, span, d), full),
            pltpu.VMEM((span, d), full),
            pltpu.VMEM((columns, span, d), half),
            pltpu.VMEM((columns, span, d), half),
            pltpu.VMEM((rows, 2, span, d), half),
            pltpu.VMEM((rows, 2, span, d), half),
            pltpu.VMEM((3, span, d), half),
            dma((6,)),
            dma((2 * rows + 4 * columns,)),
            dma((3, n_out)),
            dma((3, n_out)),
            dma((3, max(rows, columns), n_out)),
            dma((3, max(rows, columns), n_out)),
            dma((2, max(rows, columns), n_out + 1)),
            dma((2, max(rows, columns), n_out + 1)),
            dma((3,)),
            dma((3,)),
            dma((2, 3)),
        ],
        compiler_params=pltpu.CompilerParams(collective_id=0, has_side_effects=True, vmem_limit_bytes=24*1024*1024),
    )(
        stay(query_image), stay(key_image), stay(value_image), stay(attended_image), stay(upstream_image),
        stay(logsum_image.T), stay(query_text), stay(key_text), stay(value_text), stay(attended_text),
        stay(upstream_text), stay(text_lines),
    )
    return pl.pallas_call(
        tail,
        out_shape=(image_out,) * 3 + (text_out,) * 3,
        in_specs=[hbm] * 6,
        out_specs=(hbm,) * 6,
        scratch_shapes=[dma((6,))],
        compiler_params=pltpu.CompilerParams(vmem_limit_bytes=8*1024*1024),
    )(*grads)


def solution(mesh):
    tokens_spec = P(("outer", "inner"), None)
    return jax.shard_map(
        functools.partial(shards, mesh),
        mesh=mesh,
        in_specs=(tokens_spec,) * 6 + (P(None, "outer"),) * 6,
        out_specs=(tokens_spec,) * 3 + (P("inner", "outer"),) * 3,
        check_vma=False,
    )
```

```python
import functools
import math

import jax
import jax.numpy as jnp
from jax import lax
from jax.experimental import pallas as pl
from jax.experimental.pallas import tpu as pltpu
from jax.sharding import PartitionSpec as P

HEAD_DIM = 128
LANES = 128
LOG2E = math.log2(math.e)
MESH = pl.DeviceIdType.MESH


def across_rows(left, right, **options):
    return lax.dot_general(
        left, right, (((1,), (1,)), ((), ())), preferred_element_type=jnp.float32, **options
    )


def ring_steps(n_out):
    cores = 2 if n_out % 2 == 0 else 1
    chips = 2 if n_out // cores % 2 == 0 else 1
    steps = [
        (far, chip, core)
        for far in range(n_out // (cores * chips))
        for chip in range(chips)
        for core in range(cores)
    ]
    return cores, chips, sorted(steps, key=lambda s: ((s[0] > 0) + (s[1] > 0), s[2] if s[0] + s[1] else 0, s))


def kernel(
    dims,
    q_ref, k_ref, v_ref, o_ref, g_ref, l_ref,
    qt_ref, kt_ref, vt_ref, ot_ref, gt_ref, lt_ref,
    out_q, out_k, out_v, out_qt, out_kt, out_vt,
    qg, kv, key_flip, lines_in, stat_send, stat, row_stat, own_o, own_l, staged, text_o, text_l,
    dq_acc, dkv_acc, dq_own, dq_send, dq_recv, dkv_send, dkv_recv, final,
    local_sem, text_sem, in_send, in_recv, gather_send, gather_recv,
    sum_send, sum_recv, out_send, out_recv, out_local,
):
    n_out, n_in, rows, columns, tokens, block, share = dims
    span = block + share
    d = HEAD_DIM
    scale = HEAD_DIM ** (-0.5)
    o = lax.axis_index("outer")
    i = lax.axis_index("inner")

    line, place_in = i // rows, i % rows

    def row_peer(a):
        return (line + a) % columns * rows + place_in

    def column_peer(b):
        return line * rows + (place_in + b) % rows

    cores, chips, steps = ring_steps(n_out)
    core, chip, far = o % cores, o // cores % chips, o // (cores * chips)

    def stepped(k, sign):
        far_step, chip_step, core_step = steps[k]
        groups = n_out // (cores * chips)
        there = (far + sign * far_step + groups) % groups * chips
        there = (there + (chip + sign * chip_step + chips) % chips) * cores
        return there + (core + sign * core_step + cores) % cores

    def other(k):
        return stepped(k, 1)

    own_loads = [
        pltpu.make_async_copy(k_ref, staged.at[0, 0], local_sem.at[0]),
        pltpu.make_async_copy(v_ref, staged.at[0, 1], local_sem.at[1]),
        pltpu.make_async_copy(q_ref, staged.at[1, 0], local_sem.at[2]),
        pltpu.make_async_copy(g_ref, staged.at[1, 1], local_sem.at[3]),
        pltpu.make_async_copy(o_ref, own_o, local_sem.at[4]),
        pltpu.make_async_copy(l_ref, own_l, local_sem.at[5]),
    ]
    for copy in own_loads:
        copy.start()

    barrier = pltpu.get_barrier_semaphore()
    for k in range(1, n_out):
        pl.semaphore_signal(barrier, inc=1, device_id=(other(k), i), device_id_type=MESH)
    for k in range(cores):
        for a in range(1, columns):
            pl.semaphore_signal(barrier, inc=1, device_id=(other(k), row_peer(a)), device_id_type=MESH)
        for b in range(1, rows):
            pl.semaphore_signal(barrier, inc=1, device_id=(other(k), column_peer(b)), device_id_type=MESH)

    text_loads = []

    def text_load(source, target):
        copy = pltpu.make_async_copy(source, target, text_sem.at[len(text_loads)])
        copy.start()
        text_loads.append(copy)

    def share_of(ref, peer):
        return ref.at[pl.ds(pl.multiple_of(peer * share, share), share)]

    text = pl.ds(block, share)
    for b in range(rows):
        text_load(share_of(kt_ref, column_peer(b)), kv.at[b, 0, text])
        text_load(share_of(vt_ref, column_peer(b)), kv.at[b, 1, text])
    for a in range(columns):
        text_load(share_of(qt_ref, row_peer(a)), qg.at[a, 0, text])
        text_load(share_of(gt_ref, row_peer(a)), qg.at[a, 1, text])
        text_load(share_of(ot_ref, row_peer(a)), text_o.at[a])
        text_load(lt_ref.at[row_peer(a)], text_l.at[a])

    pl.semaphore_wait(barrier, n_out - 1 + cores * (columns - 1 + rows - 1))

    def piece(k):
        return pl.ds(k * tokens, tokens)

    def exchange(which, source, target, k):
        if k == 0:
            return pltpu.make_async_copy(source, target, in_recv.at[which, 0])
        return pltpu.make_async_remote_copy(
            src_ref=source,
            dst_ref=target,
            send_sem=in_send.at[which, k],
            recv_sem=in_recv.at[which, k],
            device_id=(other(k), i),
            device_id_type=MESH,
        )

    def head_of(which, k):
        return staged.at[which, :, :, pl.ds(pl.multiple_of(other(k) * d, d), d)]

    homes = (kv, qg)
    sizes = (rows, columns, columns)

    def arrival(which, k):
        if which == 2:
            return exchange(2, stat_send.at[other(k)], stat.at[0, k], k)
        return exchange(which, head_of(which, k), homes[which].at[0, :, piece(k)], k)

    def gather(which, offset, k):
        place = (sizes[which] - offset) % sizes[which]
        if which == 2:
            source, target = stat.at[0], stat.at[place]
        else:
            source = head_of(which, k) if k < cores else homes[which].at[0, :, piece(k)]
            target = homes[which].at[place, :, piece(k)]
        peer = row_peer(offset) if which else column_peer(offset)
        return pltpu.make_async_remote_copy(
            src_ref=source,
            dst_ref=target,
            send_sem=gather_send.at[which, offset, k],
            recv_sem=gather_recv.at[which, place, k],
            device_id=(other(k) if which < 2 and k < cores else o, peer),
            device_id_type=MESH,
        )

    at_end = jnp.logical_or(i == 0, i == n_in - 1)

    def ordered(first, second):
        @pl.when(at_end)
        def _():
            first()
            second()

        @pl.when(jnp.logical_not(at_end))
        def _():
            second()
            first()

    def depart(which):
        for k in range(cores):
            for offset in range(1, sizes[which]):
                gather(which, offset, k).start()
        for k in (*range(cores, n_out), *range(cores)):
            arrival(which, k).start()

    for copy in own_loads:
        copy.wait()
    ordered(lambda: depart(0), lambda: depart(1))

    lane = lax.broadcasted_iota(jnp.int32, (1, LANES), 1)
    ones = jnp.ones((8, d), jnp.float32)
    repeats = LANES // tokens
    lines_in[...] = jnp.zeros_like(lines_in)
    lines_in[:, 0:tokens] = own_l[...]
    image_lines = lines_in[...]
    for p in range(1, repeats):
        moved = pltpu.roll(lines_in[...], p * tokens, 1)
        image_lines = jnp.where(lane // tokens == p, moved, image_lines)
    image_lines = image_lines * LOG2E
    for h in range(n_out):
        cut = slice(h * d, (h + 1) * d)
        product = staged[1, 1, :, cut].astype(jnp.float32) * own_o[:, cut].astype(jnp.float32)
        product = jnp.concatenate([product] * repeats, axis=0)
        delta = across_rows(ones, product, precision=lax.Precision.HIGHEST)
        stat_send[h, 0:1, :] = image_lines[h : h + 1, :]
        stat_send[h, 1:2, :] = delta[0:1, :]
    for k in range(n_out):
        arrival(2, k).start()

    def landed(which, k):
        if k == 0:
            arrival(which, k).wait()
        else:
            arrival(which, k).wait_recv()

    def forward(which):
        for k in range(cores, n_out):
            landed(which, k)
            for offset in range(1, sizes[which]):
                gather(which, offset, k).start()

    ordered(lambda: forward(0), lambda: forward(1))
    for which in range(2):
        for k in range(cores):
            landed(which, k)
    for k in range(n_out):
        landed(2, k)
    for offset in range(1, columns):
        gather(2, offset, 0).start()

    for copy in text_loads:
        copy.wait()
    for a in range(columns):
        product = qg[a, 1, text].astype(jnp.float32) * text_o[a].astype(jnp.float32)
        delta = across_rows(ones, product, precision=lax.Precision.HIGHEST)
        row_stat[a, 0:1, text] = text_l[a] * LOG2E
        row_stat[a, 1:2, text] = delta[0:1, :]

    dq_acc[...] = jnp.zeros_like(dq_acc)
    dkv_acc[...] = jnp.zeros_like(dkv_acc)

    def spread_statistics(a):
        for start in range(0, block, LANES):
            first = start // tokens
            lines = [stat[a, first + p] for p in range(min(repeats, n_out - first))]
            merged = lines[0]
            for p in range(1, len(lines)):
                merged = jnp.where(lane // tokens == p, lines[p], merged)
            row_stat[a, :, start : start + LANES] = merged

    def flip_keys(b):
        key_flip[b] = kv[b, 0].astype(jnp.float32).T.astype(jnp.bfloat16)

    size = math.gcd(block, 256)
    chunks = [(start, size) for start in range(0, block, size)] + [(block, share)]

    def total(kind, offset, n):
        group = rows if kind else columns
        place = (group - offset) % group
        cut = piece(n) if n < n_out else text
        if kind:
            source, target = dkv_send.at[offset, :, cut], dkv_recv.at[place, :, cut]
        else:
            source, target = dq_send.at[offset, cut], dq_recv.at[place, cut]
        peer = column_peer(offset) if kind else row_peer(offset)
        return pltpu.make_async_remote_copy(
            src_ref=source,
            dst_ref=target,
            send_sem=sum_send.at[kind, offset, n],
            recv_sem=sum_recv.at[kind, place, n],
            device_id=(o, peer),
            device_id_type=MESH,
        )

    def pieces(n):
        start, length = chunks[n]
        return range(start // tokens, (start + length) // tokens) if start < block else (n_out,)

    def query_sum(a, n):
        start, length = chunks[n]
        return dq_acc[a, :, start : start + length].T * scale

    def work(a, b, n):
        start, length = chunks[n]
        cut = slice(start, start + length)
        keys, values = kv[b, 0], kv[b, 1]
        queries, upstream = qg[a, 0, cut], qg[a, 1, cut]
        scores = across_rows(keys, queries) * (scale * LOG2E)
        weights = jnp.exp2(scores - row_stat[a, 0:1, cut])
        slopes = across_rows(values, upstream)
        mixed = (weights * (slopes - row_stat[a, 1:2, cut])).astype(jnp.bfloat16)
        weights = weights.astype(jnp.bfloat16)
        dkv_acc[b, 1] += jnp.dot(weights, upstream, preferred_element_type=jnp.float32)
        dkv_acc[b, 0] += jnp.dot(mixed, queries, preferred_element_type=jnp.float32)
        dq_acc[a, :, cut] += jnp.dot(key_flip[b], mixed, preferred_element_type=jnp.float32)

    def work_keys(a, b, n):
        start, length = chunks[n]
        cut = slice(start, start + length)
        keys, values = kv[b, 0, cut], kv[b, 1, cut]
        queries, upstream = qg[a, 0], qg[a, 1]
        scores = across_rows(keys, queries) * (scale * LOG2E)
        weights = jnp.exp2(scores - row_stat[a, 0:1])
        slopes = across_rows(values, upstream)
        mixed = (weights * (slopes - row_stat[a, 1:2])).astype(jnp.bfloat16)
        weights = weights.astype(jnp.bfloat16)
        dkv_acc[b, 1, cut] += jnp.dot(weights, upstream, preferred_element_type=jnp.float32)
        dkv_acc[b, 0, cut] += jnp.dot(mixed, queries, preferred_element_type=jnp.float32)
        dq_acc[a] += jnp.dot(key_flip[b, :, cut], mixed, preferred_element_type=jnp.float32)

    spread_statistics(0)
    flip_keys(0)
    def own_tile():
        for n in range(len(chunks)):
            work(0, 0, n)

    pl.when(jnp.logical_not(at_end))(own_tile)

    def near_keys_landed(b, n):
        start, length = chunks[n]
        if start < block:
            for k in range(start // tokens, (start + length) // tokens):
                gather(0, (rows - b) % rows, k).wait_recv()
        cut = slice(start, start + length)
        key_flip[b, :, cut] = kv[b, 0, cut].astype(jnp.float32).T.astype(jnp.bfloat16)

    def far_queries_landed(a, n):
        start, length = chunks[n]
        if start < block:
            for k in range(start // tokens, (start + length) // tokens):
                gather(1, (columns - a) % columns, k).wait_recv()
        if start == 0:
            gather(2, (columns - a) % columns, 0).wait_recv()
            spread_statistics(a)

    def gathers_left(which):
        for offset in range(1, sizes[which]):
            for k in range(n_out):
                gather(which, offset, k).wait_send()

    def send_queries(a, n, order=iter):
        start, length = chunks[n]
        dq_send[a, start : start + length] = query_sum(a, n).astype(jnp.bfloat16)
        for p in order(pieces(n)):
            total(0, a, p).start()

    def send_keys(b, n, order=iter):
        start, length = chunks[n]
        cut = slice(start, start + length)
        dkv_send[b, 0, cut] = (dkv_acc[b, 0, cut] * scale).astype(jnp.bfloat16)
        dkv_send[b, 1, cut] = dkv_acc[b, 1, cut].astype(jnp.bfloat16)
        for p in order(pieces(n)):
            total(1, b, p).start()

    places = (len(chunks) - 1, *range(len(chunks) - 1))
    outward = (*reversed(range(len(chunks) - 1)), len(chunks) - 1)

    def loop(first, last, body):
        def with_carry(index, carry):
            body(index)
            return carry

        if last - first <= 2:
            for index in range(first, last):
                body(index)
        else:
            lax.fori_loop(first, last, with_carry, 0)

    @pl.when(jnp.logical_not(at_end))
    def _():
        def near_keys(b):
            for n in places:
                near_keys_landed(b, n)
            for n in places:
                work(0, b, n)

        def far_queries(a):
            for n in places[:-1]:
                far_queries_landed(a, n)
                loop(0, rows, lambda b: work(a, rows - 1 - b, n))
                send_queries(a, n)

        def give_keys(b):
            for n in outward:
                send_keys(b, n, reversed)

        def last_queries(a):
            n = places[-1]
            far_queries_landed(a, n)
            loop(1, rows, lambda b: work(a, b, n))

        def give_queries(a):
            work(a, 0, places[-1])
            send_queries(a, places[-1])

        loop(1, rows, near_keys)
        loop(1, columns, far_queries)
        loop(1, columns, last_queries)
        loop(1, rows, give_keys)
        loop(1, columns, give_queries)
        gathers_left(0)
        gathers_left(1)

    @pl.when(at_end)
    def _():
        def landed_queries(a):
            for n in places:
                far_queries_landed(a, n)

        def far_queries(a):
            for n in places:
                work(a, 0, n)

        def near_keys(group):
            def body(b):
                for n in group:
                    near_keys_landed(b, n)
                    loop(0, columns, lambda a: work_keys(a, b, n))
                    send_keys(b, n)

            return body

        def give_queries(a):
            for n in outward:
                send_queries(a, n, reversed)

        loop(1, columns, landed_queries)
        loop(1, rows, near_keys(places))
        loop(1, columns, far_queries)
        loop(1, columns, give_queries)
        own_tile()
        gathers_left(0)
        gathers_left(1)

    mine = pl.ds(pl.multiple_of(o * d, d), d)
    images, texts = (out_q, out_k, out_v), (out_qt, out_kt, out_vt)

    def out_copy(which, k):
        source, target = final.at[which, piece(k)], images[which].at[:, mine]
        if k == 0:
            return pltpu.make_async_copy(source, target, out_local.at[0, which])
        return pltpu.make_async_remote_copy(
            src_ref=source,
            dst_ref=target,
            send_sem=out_send.at[which],
            recv_sem=out_recv.at[which],
            device_id=(stepped(k, -1), i),
            device_id_type=MESH,
        )

    def text_copy(which):
        return pltpu.make_async_copy(final.at[which, text], texts[which], out_local.at[1, which])

    def give_back(which, p):
        if p < n_out:
            out_copy(which, p).start()
        else:
            text_copy(which).start()

    def finish_queries(places, order):
        for n in range(len(chunks)):
            start, length = chunks[n]
            dq_own[start : start + length] = query_sum(0, n)
        for n in places:
            for p in order(pieces(n)):
                cut = piece(p) if p < n_out else text
                grad = dq_own[cut]
                for a in range(1, columns):
                    total(0, (columns - a) % columns, p).wait_recv()
                    grad = grad + dq_recv[a, cut].astype(jnp.float32)
                final[0, cut] = grad.astype(jnp.bfloat16)
                give_back(0, p)

    def finish_keys(places, order):
        for n in places:
            for p in order(pieces(n)):
                cut = piece(p) if p < n_out else text
                for b in range(1, rows):
                    total(1, (rows - b) % rows, p).wait_recv()
                for part in (0, 1):
                    grad = dkv_acc[0, part, cut]
                    if part == 0:
                        grad = grad * scale
                    for b in range(1, rows):
                        grad = grad + dkv_recv[b, part, cut].astype(jnp.float32)
                    final[1 + part, cut] = grad.astype(jnp.bfloat16)
                    give_back(1 + part, p)

    for which in range(3):
        for k in range(1, n_out):
            arrival(which, k).wait_send()
    for a in range(1, columns):
        gather(2, a, 0).wait_send()

    @pl.when(at_end)
    def _():
        finish_queries(places, iter)
        finish_keys(outward, reversed)

    @pl.when(jnp.logical_not(at_end))
    def _():
        finish_keys(places, iter)
        finish_queries(outward, reversed)


    for n in range(n_out + 1):
        for a in range(1, columns):
            total(0, a, n).wait_send()
        for b in range(1, rows):
            total(1, b, n).wait_send()
    for which in range(3):
        text_copy(which).wait()
        out_copy(which, 0).wait()
        others = images[which].at[:, pl.ds(0, (n_out - 1) * d)]
        sent = final.at[which, pl.ds(0, (n_out - 1) * tokens)]
        pltpu.make_async_copy(sent, sent, out_send.at[which]).wait()
        pltpu.make_async_copy(others, others, out_recv.at[which]).wait()


def tail(*refs):
    copies = [pltpu.make_async_copy(s, t, refs[12].at[n]) for n, (s, t) in enumerate(zip(refs[:6], refs[6:12]))]
    for copy in copies:
        copy.start()
    for copy in copies:
        copy.wait()


def shards(
    mesh,
    query_image,
    key_image,
    value_image,
    attended_image,
    upstream_image,
    logsum_image,
    query_text,
    key_text,
    value_text,
    attended_text,
    upstream_text,
    logsum_text,
):
    n_out, n_in = mesh.shape["outer"], mesh.shape["inner"]
    rows = max(c for c in range(1, math.isqrt(n_in) + 1) if n_in % c == 0)
    columns = n_in // rows
    tokens, width = query_image.shape
    block = tokens * n_out
    share = query_text.shape[0] // n_in
    span = block + share
    d = HEAD_DIM
    text_lines = logsum_text.reshape(n_in, 1, share)
    half, full = jnp.bfloat16, jnp.float32
    dma = pltpu.SemaphoreType.DMA
    hbm = pl.BlockSpec(memory_space=pl.ANY)
    image_out = jax.ShapeDtypeStruct((tokens, width), half)
    text_out = jax.ShapeDtypeStruct((share, d), half)

    def stay(array):
        return pltpu.with_memory_space_constraint(array, pltpu.HBM)

    grads = pl.pallas_call(
        functools.partial(kernel, (n_out, n_in, rows, columns, tokens, block, share)),
        out_shape=(pltpu.VMEM((tokens, width), half),) * 3 + (pltpu.VMEM((share, d), half),) * 3,
        in_specs=[hbm] * 12,
        out_specs=(hbm,) * 6,
        scratch_shapes=[
            pltpu.VMEM((columns, 2, span, d), half),
            pltpu.VMEM((rows, 2, span, d), half),
            pltpu.VMEM((rows, d, span), half),
            pltpu.VMEM((n_out, LANES), full),
            pltpu.VMEM((n_out, 2, LANES), full),
            pltpu.VMEM((columns, n_out, 2, LANES), full),
            pltpu.VMEM((columns, 2, span), full),
            pltpu.VMEM((tokens, width), half),
            pltpu.VMEM((n_out, tokens), full),
            pltpu.VMEM((2, 2, tokens, width), half),
            pltpu.VMEM((columns, share, d), half),
            pltpu.VMEM((columns, 1, share), full),
            pltpu.VMEM((columns, d, span), full),
            pltpu.VMEM((rows, 2, span, d), full),
            pltpu.VMEM((span, d), full),
            pltpu.VMEM((columns, span, d), half),
            pltpu.VMEM((columns, span, d), half),
            pltpu.VMEM((rows, 2, span, d), half),
            pltpu.VMEM((rows, 2, span, d), half),
            pltpu.VMEM((3, span, d), half),
            dma((6,)),
            dma((2 * rows + 4 * columns,)),
            dma((3, n_out)),
            dma((3, n_out)),
            dma((3, max(rows, columns), n_out)),
            dma((3, max(rows, columns), n_out)),
            dma((2, max(rows, columns), n_out + 1)),
            dma((2, max(rows, columns), n_out + 1)),
            dma((3,)),
            dma((3,)),
            dma((2, 3)),
        ],
        compiler_params=pltpu.CompilerParams(collective_id=0, has_side_effects=True, vmem_limit_bytes=24*1024*1024),
    )(
        stay(query_image), stay(key_image), stay(value_image), stay(attended_image), stay(upstream_image),
        stay(logsum_image.T), stay(query_text), stay(key_text), stay(value_text), stay(attended_text),
        stay(upstream_text), stay(text_lines),
    )
    return pl.pallas_call(
        tail,
        out_shape=(image_out,) * 3 + (text_out,) * 3,
        in_specs=[hbm] * 6,
        out_specs=(hbm,) * 6,
        scratch_shapes=[dma((6,))],
        compiler_params=pltpu.CompilerParams(vmem_limit_bytes=8*1024*1024),
    )(*grads)


def solution(mesh):
    tokens_spec = P(("outer", "inner"), None)
    return jax.shard_map(
        functools.partial(shards, mesh),
        mesh=mesh,
        in_specs=(tokens_spec,) * 6 + (P(None, "outer"),) * 6,
        out_specs=(tokens_spec,) * 3 + (P("inner", "outer"),) * 3,
        check_vma=False,
    )
```

```python
import functools
import math

import jax
import jax.numpy as jnp
from jax import lax
from jax.experimental import pallas as pl
from jax.experimental.pallas import tpu as pltpu
from jax.sharding import PartitionSpec as P

HEAD_DIM = 128
LANES = 128
LOG2E = math.log2(math.e)
MESH = pl.DeviceIdType.MESH


def across_rows(left, right, **options):
    return lax.dot_general(
        left, right, (((1,), (1,)), ((), ())), preferred_element_type=jnp.float32, **options
    )


def ring_steps(n_out):
    cores = 2 if n_out % 2 == 0 else 1
    chips = 2 if n_out // cores % 2 == 0 else 1
    steps = [
        (far, chip, core)
        for far in range(n_out // (cores * chips))
        for chip in range(chips)
        for core in range(cores)
    ]
    return cores, chips, sorted(steps, key=lambda s: ((s[0] > 0) + (s[1] > 0), s[2] if s[0] + s[1] else 0, s))


def kernel(
    dims,
    q_ref, k_ref, v_ref, o_ref, g_ref, l_ref,
    qt_ref, kt_ref, vt_ref, ot_ref, gt_ref, lt_ref,
    out_q, out_k, out_v, out_qt, out_kt, out_vt,
    qg, kv, key_flip, lines_in, stat_send, stat, row_stat, own_o, own_l, staged, text_o, text_l,
    dq_acc, dkv_acc, dq_own, dq_send, dq_recv, dkv_send, dkv_recv, final,
    local_sem, text_sem, in_send, in_recv, gather_send, gather_recv,
    sum_send, sum_recv, out_send, out_recv, out_local,
):
    n_out, n_in, rows, columns, tokens, block, share = dims
    span = block + share
    d = HEAD_DIM
    scale = HEAD_DIM ** (-0.5)
    o = lax.axis_index("outer")
    i = lax.axis_index("inner")

    line, place_in = i // rows, i % rows

    def row_peer(a):
        return (line + a) % columns * rows + place_in

    def column_peer(b):
        return line * rows + (place_in + b) % rows

    cores, chips, steps = ring_steps(n_out)
    core, chip, far = o % cores, o // cores % chips, o // (cores * chips)

    def stepped(k, sign):
        far_step, chip_step, core_step = steps[k]
        groups = n_out // (cores * chips)
        there = (far + sign * far_step + groups) % groups * chips
        there = (there + (chip + sign * chip_step + chips) % chips) * cores
        return there + (core + sign * core_step + cores) % cores

    def other(k):
        return stepped(k, 1)

    own_loads = [
        pltpu.make_async_copy(k_ref, staged.at[0, 0], local_sem.at[0]),
        pltpu.make_async_copy(v_ref, staged.at[0, 1], local_sem.at[1]),
        pltpu.make_async_copy(q_ref, staged.at[1, 0], local_sem.at[2]),
        pltpu.make_async_copy(g_ref, staged.at[1, 1], local_sem.at[3]),
        pltpu.make_async_copy(o_ref, own_o, local_sem.at[4]),
        pltpu.make_async_copy(l_ref, own_l, local_sem.at[5]),
    ]
    for copy in own_loads:
        copy.start()

    barrier = pltpu.get_barrier_semaphore()
    for k in range(1, n_out):
        pl.semaphore_signal(barrier, inc=1, device_id=(other(k), i), device_id_type=MESH)
    for k in range(cores):
        for a in range(1, columns):
            pl.semaphore_signal(barrier, inc=1, device_id=(other(k), row_peer(a)), device_id_type=MESH)
        for b in range(1, rows):
            pl.semaphore_signal(barrier, inc=1, device_id=(other(k), column_peer(b)), device_id_type=MESH)

    text_loads = []

    def text_load(source, target):
        copy = pltpu.make_async_copy(source, target, text_sem.at[len(text_loads)])
        copy.start()
        text_loads.append(copy)

    def share_of(ref, peer):
        return ref.at[pl.ds(pl.multiple_of(peer * share, share), share)]

    text = pl.ds(block, share)
    for b in range(rows):
        text_load(share_of(kt_ref, column_peer(b)), kv.at[b, 0, text])
        text_load(share_of(vt_ref, column_peer(b)), kv.at[b, 1, text])
    for a in range(columns):
        text_load(share_of(qt_ref, row_peer(a)), qg.at[a, 0, text])
        text_load(share_of(gt_ref, row_peer(a)), qg.at[a, 1, text])
        text_load(share_of(ot_ref, row_peer(a)), text_o.at[a])
        text_load(lt_ref.at[row_peer(a)], text_l.at[a])

    pl.semaphore_wait(barrier, n_out - 1 + cores * (columns - 1 + rows - 1))

    def piece(k):
        return pl.ds(k * tokens, tokens)

    def exchange(which, source, target, k):
        if k == 0:
            return pltpu.make_async_copy(source, target, in_recv.at[which, 0])
        return pltpu.make_async_remote_copy(
            src_ref=source,
            dst_ref=target,
            send_sem=in_send.at[which, k],
            recv_sem=in_recv.at[which, k],
            device_id=(other(k), i),
            device_id_type=MESH,
        )

    def head_of(which, k):
        return staged.at[which, :, :, pl.ds(pl.multiple_of(other(k) * d, d), d)]

    homes = (kv, qg)
    sizes = (rows, columns, columns)

    def arrival(which, k):
        if which == 2:
            return exchange(2, stat_send.at[other(k)], stat.at[0, k], k)
        return exchange(which, head_of(which, k), homes[which].at[0, :, piece(k)], k)

    def gather(which, offset, k):
        place = (sizes[which] - offset) % sizes[which]
        if which == 2:
            source, target = stat.at[0], stat.at[place]
        else:
            source = head_of(which, k) if k < cores else homes[which].at[0, :, piece(k)]
            target = homes[which].at[place, :, piece(k)]
        peer = row_peer(offset) if which else column_peer(offset)
        return pltpu.make_async_remote_copy(
            src_ref=source,
            dst_ref=target,
            send_sem=gather_send.at[which, offset, k],
            recv_sem=gather_recv.at[which, place, k],
            device_id=(other(k) if which < 2 and k < cores else o, peer),
            device_id_type=MESH,
        )

    at_end = jnp.logical_or(i == 0, i == n_in - 1)

    def ordered(first, second):
        @pl.when(at_end)
        def _():
            first()
            second()

        @pl.when(jnp.logical_not(at_end))
        def _():
            second()
            first()

    def depart(which):
        for k in range(cores):
            for offset in range(1, sizes[which]):
                gather(which, offset, k).start()
        for k in (*range(cores, n_out), *range(cores)):
            arrival(which, k).start()

    for copy in own_loads:
        copy.wait()
    ordered(lambda: depart(0), lambda: depart(1))

    lane = lax.broadcasted_iota(jnp.int32, (1, LANES), 1)
    ones = jnp.ones((8, d), jnp.float32)
    repeats = LANES // tokens
    lines_in[...] = jnp.zeros_like(lines_in)
    lines_in[:, 0:tokens] = own_l[...]
    image_lines = lines_in[...]
    for p in range(1, repeats):
        moved = pltpu.roll(lines_in[...], p * tokens, 1)
        image_lines = jnp.where(lane // tokens == p, moved, image_lines)
    image_lines = image_lines * LOG2E
    for h in range(n_out):
        cut = slice(h * d, (h + 1) * d)
        product = staged[1, 1, :, cut].astype(jnp.float32) * own_o[:, cut].astype(jnp.float32)
        product = jnp.concatenate([product] * repeats, axis=0)
        delta = across_rows(ones, product, precision=lax.Precision.HIGHEST)
        stat_send[h, 0:1, :] = image_lines[h : h + 1, :]
        stat_send[h, 1:2, :] = delta[0:1, :]
    for k in range(n_out):
        arrival(2, k).start()

    def landed(which, k):
        if k == 0:
            arrival(which, k).wait()
        else:
            arrival(which, k).wait_recv()

    def forward(which):
        for k in range(cores, n_out):
            landed(which, k)
            for offset in range(1, sizes[which]):
                gather(which, offset, k).start()

    ordered(lambda: forward(0), lambda: forward(1))
    for which in range(2):
        for k in range(cores):
            landed(which, k)
    for k in range(n_out):
        landed(2, k)
    for offset in range(1, columns):
        gather(2, offset, 0).start()

    for copy in text_loads:
        copy.wait()
    for a in range(columns):
        product = qg[a, 1, text].astype(jnp.float32) * text_o[a].astype(jnp.float32)
        delta = across_rows(ones, product, precision=lax.Precision.HIGHEST)
        row_stat[a, 0:1, text] = text_l[a] * LOG2E
        row_stat[a, 1:2, text] = delta[0:1, :]

    dq_acc[...] = jnp.zeros_like(dq_acc)
    dkv_acc[...] = jnp.zeros_like(dkv_acc)

    def spread_statistics(a):
        for start in range(0, block, LANES):
            first = start // tokens
            lines = [stat[a, first + p] for p in range(min(repeats, n_out - first))]
            merged = lines[0]
            for p in range(1, len(lines)):
                merged = jnp.where(lane // tokens == p, lines[p], merged)
            row_stat[a, :, start : start + LANES] = merged

    def flip_keys(b):
        key_flip[b] = kv[b, 0].astype(jnp.float32).T.astype(jnp.bfloat16)

    size = math.gcd(block, 256)
    chunks = [(start, size) for start in range(0, block, size)] + [(block, share)]

    def total(kind, offset, n):
        group = rows if kind else columns
        place = (group - offset) % group
        cut = piece(n) if n < n_out else text
        if kind:
            source, target = dkv_send.at[offset, :, cut], dkv_recv.at[place, :, cut]
        else:
            source, target = dq_send.at[offset, cut], dq_recv.at[place, cut]
        peer = column_peer(offset) if kind else row_peer(offset)
        return pltpu.make_async_remote_copy(
            src_ref=source,
            dst_ref=target,
            send_sem=sum_send.at[kind, offset],
            recv_sem=sum_recv.at[kind, place, n],
            device_id=(o, peer),
            device_id_type=MESH,
        )

    def pieces(n):
        start, length = chunks[n]
        return range(start // tokens, (start + length) // tokens) if start < block else (n_out,)

    def query_sum(a, n):
        start, length = chunks[n]
        return dq_acc[a, :, start : start + length].T * scale

    def work(a, b, n):
        start, length = chunks[n]
        cut = slice(start, start + length)
        keys, values = kv[b, 0], kv[b, 1]
        queries, upstream = qg[a, 0, cut], qg[a, 1, cut]
        scores = across_rows(keys, queries) * (scale * LOG2E)
        weights = jnp.exp2(scores - row_stat[a, 0:1, cut])
        slopes = across_rows(values, upstream)
        mixed = (weights * (slopes - row_stat[a, 1:2, cut])).astype(jnp.bfloat16)
        weights = weights.astype(jnp.bfloat16)
        dkv_acc[b, 1] += jnp.dot(weights, upstream, preferred_element_type=jnp.float32)
        dkv_acc[b, 0] += jnp.dot(mixed, queries, preferred_element_type=jnp.float32)
        dq_acc[a, :, cut] += jnp.dot(key_flip[b], mixed, preferred_element_type=jnp.float32)

    def work_keys(a, b, n):
        start, length = chunks[n]
        cut = slice(start, start + length)
        keys, values = kv[b, 0, cut], kv[b, 1, cut]
        queries, upstream = qg[a, 0], qg[a, 1]
        scores = across_rows(keys, queries) * (scale * LOG2E)
        weights = jnp.exp2(scores - row_stat[a, 0:1])
        slopes = across_rows(values, upstream)
        mixed = (weights * (slopes - row_stat[a, 1:2])).astype(jnp.bfloat16)
        weights = weights.astype(jnp.bfloat16)
        dkv_acc[b, 1, cut] += jnp.dot(weights, upstream, preferred_element_type=jnp.float32)
        dkv_acc[b, 0, cut] += jnp.dot(mixed, queries, preferred_element_type=jnp.float32)
        dq_acc[a] += jnp.dot(key_flip[b, :, cut], mixed, preferred_element_type=jnp.float32)

    spread_statistics(0)
    flip_keys(0)
    def own_tile():
        for n in range(len(chunks)):
            work(0, 0, n)

    pl.when(jnp.logical_not(at_end))(own_tile)

    def near_keys_landed(b, n):
        start, length = chunks[n]
        if start < block:
            for k in range(start // tokens, (start + length) // tokens):
                gather(0, (rows - b) % rows, k).wait_recv()
        cut = slice(start, start + length)
        key_flip[b, :, cut] = kv[b, 0, cut].astype(jnp.float32).T.astype(jnp.bfloat16)

    def far_queries_landed(a, n):
        start, length = chunks[n]
        if start < block:
            for k in range(start // tokens, (start + length) // tokens):
                gather(1, (columns - a) % columns, k).wait_recv()
        if start == 0:
            gather(2, (columns - a) % columns, 0).wait_recv()
            spread_statistics(a)

    def gathers_left(which):
        for offset in range(1, sizes[which]):
            for k in range(n_out):
                gather(which, offset, k).wait_send()

    def send_queries(a, n, order=iter):
        start, length = chunks[n]
        dq_send[a, start : start + length] = query_sum(a, n).astype(jnp.bfloat16)
        for p in order(pieces(n)):
            total(0, a, p).start()

    def send_keys(b, n, order=iter):
        start, length = chunks[n]
        cut = slice(start, start + length)
        dkv_send[b, 0, cut] = (dkv_acc[b, 0, cut] * scale).astype(jnp.bfloat16)
        dkv_send[b, 1, cut] = dkv_acc[b, 1, cut].astype(jnp.bfloat16)
        for p in order(pieces(n)):
            total(1, b, p).start()

    places = (len(chunks) - 1, *range(len(chunks) - 1))
    outward = (*reversed(range(len(chunks) - 1)), len(chunks) - 1)

    def loop(first, last, body):
        def with_carry(index, carry):
            body(index)
            return carry

        if last - first <= 2:
            for index in range(first, last):
                body(index)
        else:
            lax.fori_loop(first, last, with_carry, 0)

    @pl.when(jnp.logical_not(at_end))
    def _():
        def near_keys(b):
            for n in places:
                near_keys_landed(b, n)
            for n in places:
                work(0, b, n)

        def far_queries(a):
            for n in places[:-1]:
                far_queries_landed(a, n)
                loop(0, rows, lambda b: work(a, rows - 1 - b, n))
                send_queries(a, n)

        def give_keys(group):
            def body(b):
                for n in group:
                    send_keys(b, n, reversed)

            return body

        def last_queries(a):
            n = places[-1]
            far_queries_landed(a, n)
            loop(1, rows, lambda b: work(a, b, n))

        def give_queries(a):
            work(a, 0, places[-1])
            send_queries(a, places[-1])

        loop(1, rows, near_keys)
        loop(1, columns, far_queries)
        loop(1, columns, last_queries)
        loop(1, rows, give_keys(outward[:1]))
        loop(1, columns, give_queries)
        loop(1, rows, give_keys(outward[1:]))
        gathers_left(0)
        gathers_left(1)

    @pl.when(at_end)
    def _():
        def landed_queries(a):
            for n in places:
                far_queries_landed(a, n)

        def far_queries(a):
            for n in places:
                work(a, 0, n)

        def near_keys(group):
            def body(b):
                for n in group:
                    near_keys_landed(b, n)
                    loop(0, columns, lambda a: work_keys(a, b, n))
                    send_keys(b, n)

            return body

        def give_queries(a):
            for n in outward:
                send_queries(a, n, reversed)

        loop(1, columns, landed_queries)
        loop(1, rows, near_keys(places))
        loop(1, columns, far_queries)
        loop(1, columns, give_queries)
        own_tile()
        gathers_left(0)
        gathers_left(1)

    mine = pl.ds(pl.multiple_of(o * d, d), d)
    images, texts = (out_q, out_k, out_v), (out_qt, out_kt, out_vt)

    def out_copy(which, k):
        source, target = final.at[which, piece(k)], images[which].at[:, mine]
        if k == 0:
            return pltpu.make_async_copy(source, target, out_local.at[0, which])
        return pltpu.make_async_remote_copy(
            src_ref=source,
            dst_ref=target,
            send_sem=out_send.at[which],
            recv_sem=out_recv.at[which],
            device_id=(stepped(k, -1), i),
            device_id_type=MESH,
        )

    def text_copy(which):
        return pltpu.make_async_copy(final.at[which, text], texts[which], out_local.at[1, which])

    def give_back(which, p):
        if p < n_out:
            out_copy(which, p).start()
        else:
            texts[which][...] = final[which, text]

    def finish_queries(places, order):
        for n in range(len(chunks)):
            start, length = chunks[n]
            dq_own[start : start + length] = query_sum(0, n)
        for n in places:
            for p in order(pieces(n)):
                cut = piece(p) if p < n_out else text
                grad = dq_own[cut]
                for a in range(1, columns):
                    total(0, (columns - a) % columns, p).wait_recv()
                    grad = grad + dq_recv[a, cut].astype(jnp.float32)
                final[0, cut] = grad.astype(jnp.bfloat16)
                give_back(0, p)

    def finish_keys(places, order):
        for n in places:
            for p in order(pieces(n)):
                cut = piece(p) if p < n_out else text
                for b in range(1, rows):
                    total(1, (rows - b) % rows, p).wait_recv()
                for part in (0, 1):
                    grad = dkv_acc[0, part, cut]
                    if part == 0:
                        grad = grad * scale
                    for b in range(1, rows):
                        grad = grad + dkv_recv[b, part, cut].astype(jnp.float32)
                    final[1 + part, cut] = grad.astype(jnp.bfloat16)
                    give_back(1 + part, p)

    for which in range(3):
        for k in range(1, n_out):
            arrival(which, k).wait_send()
    for a in range(1, columns):
        gather(2, a, 0).wait_send()

    @pl.when(at_end)
    def _():
        finish_queries(places, iter)
        finish_keys(outward, reversed)

    @pl.when(jnp.logical_not(at_end))
    def _():
        finish_keys(places, iter)
        finish_queries(outward, reversed)


    for a in range(1, columns):
        pltpu.make_async_copy(dq_send.at[a], dq_send.at[a], sum_send.at[0, a]).wait()
    for b in range(1, rows):
        pltpu.make_async_copy(dkv_send.at[b], dkv_send.at[b], sum_send.at[1, b]).wait()
    for which in range(3):
        out_copy(which, 0).wait()
        others = images[which].at[:, pl.ds(0, (n_out - 1) * d)]
        sent = final.at[which, pl.ds(0, (n_out - 1) * tokens)]
        pltpu.make_async_copy(sent, sent, out_send.at[which]).wait()
        pltpu.make_async_copy(others, others, out_recv.at[which]).wait()


def tail(*refs):
    copies = [pltpu.make_async_copy(s, t, refs[12].at[n]) for n, (s, t) in enumerate(zip(refs[:6], refs[6:12]))]
    for copy in copies:
        copy.start()
    for copy in copies:
        copy.wait()


def shards(
    mesh,
    query_image,
    key_image,
    value_image,
    attended_image,
    upstream_image,
    logsum_image,
    query_text,
    key_text,
    value_text,
    attended_text,
    upstream_text,
    logsum_text,
):
    n_out, n_in = mesh.shape["outer"], mesh.shape["inner"]
    rows = max(c for c in range(1, math.isqrt(n_in) + 1) if n_in % c == 0)
    columns = n_in // rows
    tokens, width = query_image.shape
    block = tokens * n_out
    share = query_text.shape[0] // n_in
    span = block + share
    d = HEAD_DIM
    text_lines = logsum_text.reshape(n_in, 1, share)
    half, full = jnp.bfloat16, jnp.float32
    dma = pltpu.SemaphoreType.DMA
    hbm = pl.BlockSpec(memory_space=pl.ANY)
    image_out = jax.ShapeDtypeStruct((tokens, width), half)
    text_out = jax.ShapeDtypeStruct((share, d), half)

    def stay(array):
        return pltpu.with_memory_space_constraint(array, pltpu.HBM)

    grads = pl.pallas_call(
        functools.partial(kernel, (n_out, n_in, rows, columns, tokens, block, share)),
        out_shape=(pltpu.VMEM((tokens, width), half),) * 3 + (pltpu.VMEM((share, d), half),) * 3,
        in_specs=[hbm] * 12,
        out_specs=(hbm,) * 3 + (pl.BlockSpec(memory_space=pltpu.VMEM),) * 3,
        scratch_shapes=[
            pltpu.VMEM((columns, 2, span, d), half),
            pltpu.VMEM((rows, 2, span, d), half),
            pltpu.VMEM((rows, d, span), half),
            pltpu.VMEM((n_out, LANES), full),
            pltpu.VMEM((n_out, 2, LANES), full),
            pltpu.VMEM((columns, n_out, 2, LANES), full),
            pltpu.VMEM((columns, 2, span), full),
            pltpu.VMEM((tokens, width), half),
            pltpu.VMEM((n_out, tokens), full),
            pltpu.VMEM((2, 2, tokens, width), half),
            pltpu.VMEM((columns, share, d), half),
            pltpu.VMEM((columns, 1, share), full),
            pltpu.VMEM((columns, d, span), full),
            pltpu.VMEM((rows, 2, span, d), full),
            pltpu.VMEM((span, d), full),
            pltpu.VMEM((columns, span, d), half),
            pltpu.VMEM((columns, span, d), half),
            pltpu.VMEM((rows, 2, span, d), half),
            pltpu.VMEM((rows, 2, span, d), half),
            pltpu.VMEM((3, span, d), half),
            dma((6,)),
            dma((2 * rows + 4 * columns,)),
            dma((3, n_out)),
            dma((3, n_out)),
            dma((3, max(rows, columns), n_out)),
            dma((3, max(rows, columns), n_out)),
            dma((2, max(rows, columns))),
            dma((2, max(rows, columns), n_out + 1)),
            dma((3,)),
            dma((3,)),
            dma((2, 3)),
        ],
        compiler_params=pltpu.CompilerParams(collective_id=0, has_side_effects=True, vmem_limit_bytes=24*1024*1024),
    )(
        stay(query_image), stay(key_image), stay(value_image), stay(attended_image), stay(upstream_image),
        stay(logsum_image.T), stay(query_text), stay(key_text), stay(value_text), stay(attended_text),
        stay(upstream_text), stay(text_lines),
    )
    return pl.pallas_call(
        tail,
        out_shape=(image_out,) * 3 + (text_out,) * 3,
        in_specs=[hbm] * 6,
        out_specs=(hbm,) * 6,
        scratch_shapes=[dma((6,))],
        compiler_params=pltpu.CompilerParams(vmem_limit_bytes=8*1024*1024),
    )(*grads)


def solution(mesh):
    tokens_spec = P(("outer", "inner"), None)
    return jax.shard_map(
        functools.partial(shards, mesh),
        mesh=mesh,
        in_specs=(tokens_spec,) * 6 + (P(None, "outer"),) * 6,
        out_specs=(tokens_spec,) * 3 + (P("inner", "outer"),) * 3,
        check_vma=False,
    )
```

```python
import functools
import math

import jax
import jax.numpy as jnp
from jax import lax
from jax.experimental import pallas as pl
from jax.experimental.pallas import tpu as pltpu
from jax.sharding import PartitionSpec as P

HEAD_DIM = 128
LANES = 128
LOG2E = math.log2(math.e)
MESH = pl.DeviceIdType.MESH


def across_rows(left, right, **options):
    return lax.dot_general(
        left, right, (((1,), (1,)), ((), ())), preferred_element_type=jnp.float32, **options
    )


def ring_steps(n_out):
    cores = 2 if n_out % 2 == 0 else 1
    chips = 2 if n_out // cores % 2 == 0 else 1
    steps = [
        (far, chip, core)
        for far in range(n_out // (cores * chips))
        for chip in range(chips)
        for core in range(cores)
    ]
    return cores, chips, sorted(steps, key=lambda s: ((s[0] > 0) + (s[1] > 0), s[2] if s[0] + s[1] else 0, s))


def kernel(
    dims,
    q_ref, k_ref, v_ref, o_ref, g_ref, l_ref,
    qt_ref, kt_ref, vt_ref, ot_ref, gt_ref, lt_ref,
    out_q, out_k, out_v, out_qt, out_kt, out_vt,
    qg, kv, key_flip, lines_in, stat_send, stat, row_stat, own_o, own_l, staged, text_o, text_l,
    dq_acc, dkv_acc, dq_own, dq_send, dq_recv, dkv_send, dkv_recv, final,
    local_sem, text_sem, in_send, in_recv, gather_send, gather_recv,
    sum_send, sum_recv, out_send, out_recv, out_local,
):
    n_out, n_in, rows, columns, tokens, block, share = dims
    span = block + share
    d = HEAD_DIM
    scale = HEAD_DIM ** (-0.5)
    o = lax.axis_index("outer")
    i = lax.axis_index("inner")

    line, place_in = i // rows, i % rows

    def row_peer(a):
        return (line + a) % columns * rows + place_in

    def column_peer(b):
        return line * rows + (place_in + b) % rows

    cores, chips, steps = ring_steps(n_out)
    core, chip, far = o % cores, o // cores % chips, o // (cores * chips)

    def stepped(k, sign):
        far_step, chip_step, core_step = steps[k]
        groups = n_out // (cores * chips)
        there = (far + sign * far_step + groups) % groups * chips
        there = (there + (chip + sign * chip_step + chips) % chips) * cores
        return there + (core + sign * core_step + cores) % cores

    def other(k):
        return stepped(k, 1)

    own_loads = [
        pltpu.make_async_copy(k_ref, staged.at[0, 0], local_sem.at[0]),
        pltpu.make_async_copy(v_ref, staged.at[0, 1], local_sem.at[1]),
        pltpu.make_async_copy(q_ref, staged.at[1, 0], local_sem.at[2]),
        pltpu.make_async_copy(g_ref, staged.at[1, 1], local_sem.at[3]),
        pltpu.make_async_copy(o_ref, own_o, local_sem.at[4]),
        pltpu.make_async_copy(l_ref, own_l, local_sem.at[5]),
    ]
    for copy in own_loads:
        copy.start()

    barrier = pltpu.get_barrier_semaphore()
    for k in range(1, n_out):
        pl.semaphore_signal(barrier, inc=1, device_id=(other(k), i), device_id_type=MESH)
    for k in range(cores):
        for a in range(1, columns):
            pl.semaphore_signal(barrier, inc=1, device_id=(other(k), row_peer(a)), device_id_type=MESH)
        for b in range(1, rows):
            pl.semaphore_signal(barrier, inc=1, device_id=(other(k), column_peer(b)), device_id_type=MESH)

    text_loads = []

    def text_load(source, target):
        copy = pltpu.make_async_copy(source, target, text_sem.at[len(text_loads)])
        copy.start()
        text_loads.append(copy)

    def share_of(ref, peer):
        return ref.at[pl.ds(pl.multiple_of(peer * share, share), share)]

    text = pl.ds(block, share)
    for b in range(rows):
        text_load(share_of(kt_ref, column_peer(b)), kv.at[b, 0, text])
        text_load(share_of(vt_ref, column_peer(b)), kv.at[b, 1, text])
    for a in range(columns):
        text_load(share_of(qt_ref, row_peer(a)), qg.at[a, 0, text])
        text_load(share_of(gt_ref, row_peer(a)), qg.at[a, 1, text])
        text_load(share_of(ot_ref, row_peer(a)), text_o.at[a])
        text_load(lt_ref.at[row_peer(a)], text_l.at[a])

    pl.semaphore_wait(barrier, n_out - 1 + cores * (columns - 1 + rows - 1))

    def piece(k):
        return pl.ds(k * tokens, tokens)

    def exchange(which, source, target, k):
        if k == 0:
            return pltpu.make_async_copy(source, target, in_recv.at[which, 0])
        return pltpu.make_async_remote_copy(
            src_ref=source,
            dst_ref=target,
            send_sem=in_send.at[which, k],
            recv_sem=in_recv.at[which, k],
            device_id=(other(k), i),
            device_id_type=MESH,
        )

    def head_of(which, k):
        return staged.at[which, :, :, pl.ds(pl.multiple_of(other(k) * d, d), d)]

    homes = (kv, qg)
    sizes = (rows, columns, columns)

    def arrival(which, k):
        if which == 2:
            return exchange(2, stat_send.at[other(k)], stat.at[0, k], k)
        return exchange(which, head_of(which, k), homes[which].at[0, :, piece(k)], k)

    def gather(which, offset, k):
        place = (sizes[which] - offset) % sizes[which]
        if which == 2:
            source, target = stat.at[0], stat.at[place]
        else:
            source = head_of(which, k) if k < cores else homes[which].at[0, :, piece(k)]
            target = homes[which].at[place, :, piece(k)]
        peer = row_peer(offset) if which else column_peer(offset)
        return pltpu.make_async_remote_copy(
            src_ref=source,
            dst_ref=target,
            send_sem=gather_send.at[which, offset, k],
            recv_sem=gather_recv.at[which, place, k],
            device_id=(other(k) if which < 2 and k < cores else o, peer),
            device_id_type=MESH,
        )

    at_end = jnp.logical_or(i == 0, i == n_in - 1)

    def ordered(first, second):
        @pl.when(at_end)
        def _():
            first()
            second()

        @pl.when(jnp.logical_not(at_end))
        def _():
            second()
            first()

    def depart(which):
        for k in range(cores):
            for offset in range(1, sizes[which]):
                gather(which, offset, k).start()
        for k in (*range(cores, n_out), *range(cores)):
            arrival(which, k).start()

    for copy in own_loads:
        copy.wait()
    ordered(lambda: depart(0), lambda: depart(1))

    lane = lax.broadcasted_iota(jnp.int32, (1, LANES), 1)
    ones = jnp.ones((8, d), jnp.float32)
    repeats = LANES // tokens
    lines_in[...] = jnp.zeros_like(lines_in)
    lines_in[:, 0:tokens] = own_l[...]
    image_lines = lines_in[...]
    for p in range(1, repeats):
        moved = pltpu.roll(lines_in[...], p * tokens, 1)
        image_lines = jnp.where(lane // tokens == p, moved, image_lines)
    image_lines = image_lines * LOG2E
    for h in range(n_out):
        cut = slice(h * d, (h + 1) * d)
        product = staged[1, 1, :, cut].astype(jnp.float32) * own_o[:, cut].astype(jnp.float32)
        product = jnp.concatenate([product] * repeats, axis=0)
        delta = across_rows(ones, product, precision=lax.Precision.HIGHEST)
        stat_send[h, 0:1, :] = image_lines[h : h + 1, :]
        stat_send[h, 1:2, :] = delta[0:1, :]
    for k in range(n_out):
        arrival(2, k).start()

    def landed(which, k):
        if k == 0:
            arrival(which, k).wait()
        else:
            arrival(which, k).wait_recv()

    def forward(which):
        for k in range(cores, n_out):
            landed(which, k)
            for offset in range(1, sizes[which]):
                gather(which, offset, k).start()

    ordered(lambda: forward(0), lambda: forward(1))
    for which in range(2):
        for k in range(cores):
            landed(which, k)
    for k in range(n_out):
        landed(2, k)
    for offset in range(1, columns):
        gather(2, offset, 0).start()

    for copy in text_loads:
        copy.wait()
    for a in range(columns):
        product = qg[a, 1, text].astype(jnp.float32) * text_o[a].astype(jnp.float32)
        delta = across_rows(ones, product, precision=lax.Precision.HIGHEST)
        row_stat[a, 0:1, text] = text_l[a] * LOG2E
        row_stat[a, 1:2, text] = delta[0:1, :]

    dq_acc[...] = jnp.zeros_like(dq_acc)
    dkv_acc[...] = jnp.zeros_like(dkv_acc)

    def spread_statistics(a):
        for start in range(0, block, LANES):
            first = start // tokens
            lines = [stat[a, first + p] for p in range(min(repeats, n_out - first))]
            merged = lines[0]
            for p in range(1, len(lines)):
                merged = jnp.where(lane // tokens == p, lines[p], merged)
            row_stat[a, :, start : start + LANES] = merged

    def flip_keys(b):
        key_flip[b] = kv[b, 0].astype(jnp.float32).T.astype(jnp.bfloat16)

    size = math.gcd(block, 256)
    chunks = [(start, size) for start in range(0, block, size)] + [(block, share)]

    def total(kind, offset, n):
        group = rows if kind else columns
        place = (group - offset) % group
        cut = piece(n) if n < n_out else text
        if kind:
            source, target = dkv_send.at[offset, :, cut], dkv_recv.at[place, :, cut]
        else:
            source, target = dq_send.at[offset, cut], dq_recv.at[place, cut]
        peer = column_peer(offset) if kind else row_peer(offset)
        return pltpu.make_async_remote_copy(
            src_ref=source,
            dst_ref=target,
            send_sem=sum_send.at[kind, offset],
            recv_sem=sum_recv.at[kind, place, n],
            device_id=(o, peer),
            device_id_type=MESH,
        )

    def pieces(n):
        start, length = chunks[n]
        return range(start // tokens, (start + length) // tokens) if start < block else (n_out,)

    def query_sum(a, n):
        start, length = chunks[n]
        return dq_acc[a, :, start : start + length].T * scale

    def work(a, b, n):
        start, length = chunks[n]
        cut = slice(start, start + length)
        keys, values = kv[b, 0], kv[b, 1]
        queries, upstream = qg[a, 0, cut], qg[a, 1, cut]
        scores = across_rows(keys, queries) * (scale * LOG2E)
        weights = jnp.exp2(scores - row_stat[a, 0:1, cut])
        slopes = across_rows(values, upstream)
        mixed = (weights * (slopes - row_stat[a, 1:2, cut])).astype(jnp.bfloat16)
        weights = weights.astype(jnp.bfloat16)
        dkv_acc[b, 1] += jnp.dot(weights, upstream, preferred_element_type=jnp.float32)
        dkv_acc[b, 0] += jnp.dot(mixed, queries, preferred_element_type=jnp.float32)
        dq_acc[a, :, cut] += jnp.dot(key_flip[b], mixed, preferred_element_type=jnp.float32)

    def work_keys(a, b, n):
        start, length = chunks[n]
        cut = slice(start, start + length)
        keys, values = kv[b, 0, cut], kv[b, 1, cut]
        queries, upstream = qg[a, 0], qg[a, 1]
        scores = across_rows(keys, queries) * (scale * LOG2E)
        weights = jnp.exp2(scores - row_stat[a, 0:1])
        slopes = across_rows(values, upstream)
        mixed = (weights * (slopes - row_stat[a, 1:2])).astype(jnp.bfloat16)
        weights = weights.astype(jnp.bfloat16)
        dkv_acc[b, 1, cut] += jnp.dot(weights, upstream, preferred_element_type=jnp.float32)
        dkv_acc[b, 0, cut] += jnp.dot(mixed, queries, preferred_element_type=jnp.float32)
        dq_acc[a] += jnp.dot(key_flip[b, :, cut], mixed, preferred_element_type=jnp.float32)

    spread_statistics(0)
    flip_keys(0)
    def own_tile():
        for n in range(len(chunks)):
            work(0, 0, n)

    pl.when(jnp.logical_not(at_end))(own_tile)

    def near_keys_landed(b, n):
        start, length = chunks[n]
        if start < block:
            for k in range(start // tokens, (start + length) // tokens):
                gather(0, (rows - b) % rows, k).wait_recv()
        cut = slice(start, start + length)
        key_flip[b, :, cut] = kv[b, 0, cut].astype(jnp.float32).T.astype(jnp.bfloat16)

    def far_queries_landed(a, n):
        start, length = chunks[n]
        if start < block:
            for k in range(start // tokens, (start + length) // tokens):
                gather(1, (columns - a) % columns, k).wait_recv()
        if start == 0:
            gather(2, (columns - a) % columns, 0).wait_recv()
            spread_statistics(a)

    def gathers_left(which):
        for offset in range(1, sizes[which]):
            for k in range(n_out):
                gather(which, offset, k).wait_send()

    def send_queries(a, n, order=iter):
        start, length = chunks[n]
        dq_send[a, start : start + length] = query_sum(a, n).astype(jnp.bfloat16)
        for p in order(pieces(n)):
            total(0, a, p).start()

    def send_keys(b, n, order=iter):
        start, length = chunks[n]
        cut = slice(start, start + length)
        dkv_send[b, 0, cut] = (dkv_acc[b, 0, cut] * scale).astype(jnp.bfloat16)
        dkv_send[b, 1, cut] = dkv_acc[b, 1, cut].astype(jnp.bfloat16)
        for p in order(pieces(n)):
            total(1, b, p).start()

    places = (len(chunks) - 1, *range(len(chunks) - 1))
    outward = (*reversed(range(len(chunks) - 1)), len(chunks) - 1)

    def loop(first, last, body):
        def with_carry(index, carry):
            body(index)
            return carry

        if last - first <= 2:
            for index in range(first, last):
                body(index)
        else:
            lax.fori_loop(first, last, with_carry, 0)

    @pl.when(jnp.logical_not(at_end))
    def _():
        def near_keys(b):
            for n in places:
                near_keys_landed(b, n)
            for n in places:
                work(0, b, n)

        def far_queries(a):
            for n in places[:-1]:
                far_queries_landed(a, n)
                loop(0, rows, lambda b: work(a, rows - 1 - b, n))
                send_queries(a, n)

        def give_keys(group):
            def body(b):
                for n in group:
                    send_keys(b, n, reversed)

            return body

        def last_queries(a):
            n = places[-1]
            far_queries_landed(a, n)
            loop(1, rows, lambda b: work(a, b, n))

        def give_queries(a):
            work(a, 0, places[-1])
            send_queries(a, places[-1])

        loop(1, rows, near_keys)
        loop(1, columns, far_queries)
        loop(1, columns, last_queries)
        loop(1, rows, give_keys(outward[:1]))
        loop(1, columns, give_queries)
        loop(1, rows, give_keys(outward[1:]))
        gathers_left(0)
        gathers_left(1)

    @pl.when(at_end)
    def _():
        def landed_queries(a):
            for n in places:
                far_queries_landed(a, n)

        def far_queries(a):
            for n in places:
                work(a, 0, n)

        def near_keys(group):
            def body(b):
                for n in group:
                    near_keys_landed(b, n)
                    loop(0, columns, lambda a: work_keys(a, b, n))
                    send_keys(b, n)

            return body

        def give_queries(a):
            for n in outward:
                send_queries(a, n, reversed)

        loop(1, columns, landed_queries)
        loop(1, rows, near_keys(places))
        loop(1, columns, far_queries)
        loop(1, columns, give_queries)
        own_tile()
        gathers_left(0)
        gathers_left(1)

    mine = pl.ds(pl.multiple_of(o * d, d), d)
    images, texts = (out_q, out_k, out_v), (out_qt, out_kt, out_vt)

    def out_copy(which, k):
        source, target = final.at[which, piece(k)], images[which].at[:, mine]
        if k == 0:
            return pltpu.make_async_copy(source, target, out_local.at[0, which])
        return pltpu.make_async_remote_copy(
            src_ref=source,
            dst_ref=target,
            send_sem=out_send.at[which],
            recv_sem=out_recv.at[which],
            device_id=(stepped(k, -1), i),
            device_id_type=MESH,
        )

    def text_copy(which):
        return pltpu.make_async_copy(final.at[which, text], texts[which], out_local.at[1, which])

    def give_back(which, p):
        if p < n_out:
            out_copy(which, p).start()
        else:
            texts[which][...] = final[which, text]

    for n in range(len(chunks)):
        start, length = chunks[n]
        dq_own[start : start + length] = query_sum(0, n)

    def finish_queries(places, order):
        for n in places:
            for p in order(pieces(n)):
                cut = piece(p) if p < n_out else text
                grad = dq_own[cut]
                for a in range(1, columns):
                    total(0, (columns - a) % columns, p).wait_recv()
                    grad = grad + dq_recv[a, cut].astype(jnp.float32)
                final[0, cut] = grad.astype(jnp.bfloat16)
                give_back(0, p)

    def finish_keys(places, order):
        for n in places:
            for p in order(pieces(n)):
                cut = piece(p) if p < n_out else text
                for b in range(1, rows):
                    total(1, (rows - b) % rows, p).wait_recv()
                for part in (0, 1):
                    grad = dkv_acc[0, part, cut]
                    if part == 0:
                        grad = grad * scale
                    for b in range(1, rows):
                        grad = grad + dkv_recv[b, part, cut].astype(jnp.float32)
                    final[1 + part, cut] = grad.astype(jnp.bfloat16)
                    give_back(1 + part, p)

    for which in range(3):
        for k in range(1, n_out):
            arrival(which, k).wait_send()
    for a in range(1, columns):
        gather(2, a, 0).wait_send()

    @pl.when(at_end)
    def _():
        finish_queries(places[:-1], iter)
        finish_keys(outward[:1], reversed)
        finish_queries(places[-1:], iter)
        finish_keys(outward[1:], reversed)

    @pl.when(jnp.logical_not(at_end))
    def _():
        finish_keys(places, iter)
        finish_queries(outward, reversed)


    for a in range(1, columns):
        pltpu.make_async_copy(dq_send.at[a], dq_send.at[a], sum_send.at[0, a]).wait()
    for b in range(1, rows):
        pltpu.make_async_copy(dkv_send.at[b], dkv_send.at[b], sum_send.at[1, b]).wait()
    for which in range(3):
        out_copy(which, 0).wait()
        others = images[which].at[:, pl.ds(0, (n_out - 1) * d)]
        sent = final.at[which, pl.ds(0, (n_out - 1) * tokens)]
        pltpu.make_async_copy(sent, sent, out_send.at[which]).wait()
        pltpu.make_async_copy(others, others, out_recv.at[which]).wait()


def tail(*refs):
    copies = [pltpu.make_async_copy(s, t, refs[12].at[n]) for n, (s, t) in enumerate(zip(refs[:6], refs[6:12]))]
    for copy in copies:
        copy.start()
    for copy in copies:
        copy.wait()


def shards(
    mesh,
    query_image,
    key_image,
    value_image,
    attended_image,
    upstream_image,
    logsum_image,
    query_text,
    key_text,
    value_text,
    attended_text,
    upstream_text,
    logsum_text,
):
    n_out, n_in = mesh.shape["outer"], mesh.shape["inner"]
    rows = max(c for c in range(1, math.isqrt(n_in) + 1) if n_in % c == 0)
    columns = n_in // rows
    tokens, width = query_image.shape
    block = tokens * n_out
    share = query_text.shape[0] // n_in
    span = block + share
    d = HEAD_DIM
    text_lines = logsum_text.reshape(n_in, 1, share)
    half, full = jnp.bfloat16, jnp.float32
    dma = pltpu.SemaphoreType.DMA
    hbm = pl.BlockSpec(memory_space=pl.ANY)
    image_out = jax.ShapeDtypeStruct((tokens, width), half)
    text_out = jax.ShapeDtypeStruct((share, d), half)

    def stay(array):
        return pltpu.with_memory_space_constraint(array, pltpu.HBM)

    grads = pl.pallas_call(
        functools.partial(kernel, (n_out, n_in, rows, columns, tokens, block, share)),
        out_shape=(pltpu.VMEM((tokens, width), half),) * 3 + (pltpu.VMEM((share, d), half),) * 3,
        in_specs=[hbm] * 12,
        out_specs=(hbm,) * 3 + (pl.BlockSpec(memory_space=pltpu.VMEM),) * 3,
        scratch_shapes=[
            pltpu.VMEM((columns, 2, span, d), half),
            pltpu.VMEM((rows, 2, span, d), half),
            pltpu.VMEM((rows, d, span), half),
            pltpu.VMEM((n_out, LANES), full),
            pltpu.VMEM((n_out, 2, LANES), full),
            pltpu.VMEM((columns, n_out, 2, LANES), full),
            pltpu.VMEM((columns, 2, span), full),
            pltpu.VMEM((tokens, width), half),
            pltpu.VMEM((n_out, tokens), full),
            pltpu.VMEM((2, 2, tokens, width), half),
            pltpu.VMEM((columns, share, d), half),
            pltpu.VMEM((columns, 1, share), full),
            pltpu.VMEM((columns, d, span), full),
            pltpu.VMEM((rows, 2, span, d), full),
            pltpu.VMEM((span, d), full),
            pltpu.VMEM((columns, span, d), half),
            pltpu.VMEM((columns, span, d), half),
            pltpu.VMEM((rows, 2, span, d), half),
            pltpu.VMEM((rows, 2, span, d), half),
            pltpu.VMEM((3, span, d), half),
            dma((6,)),
            dma((2 * rows + 4 * columns,)),
            dma((3, n_out)),
            dma((3, n_out)),
            dma((3, max(rows, columns), n_out)),
            dma((3, max(rows, columns), n_out)),
            dma((2, max(rows, columns))),
            dma((2, max(rows, columns), n_out + 1)),
            dma((3,)),
            dma((3,)),
            dma((2, 3)),
        ],
        compiler_params=pltpu.CompilerParams(collective_id=0, has_side_effects=True, vmem_limit_bytes=24*1024*1024),
    )(
        stay(query_image), stay(key_image), stay(value_image), stay(attended_image), stay(upstream_image),
        stay(logsum_image.T), stay(query_text), stay(key_text), stay(value_text), stay(attended_text),
        stay(upstream_text), stay(text_lines),
    )
    return pl.pallas_call(
        tail,
        out_shape=(image_out,) * 3 + (text_out,) * 3,
        in_specs=[hbm] * 6,
        out_specs=(hbm,) * 6,
        scratch_shapes=[dma((6,))],
        compiler_params=pltpu.CompilerParams(vmem_limit_bytes=8*1024*1024),
    )(*grads)


def solution(mesh):
    tokens_spec = P(("outer", "inner"), None)
    return jax.shard_map(
        functools.partial(shards, mesh),
        mesh=mesh,
        in_specs=(tokens_spec,) * 6 + (P(None, "outer"),) * 6,
        out_specs=(tokens_spec,) * 3 + (P("inner", "outer"),) * 3,
        check_vma=False,
    )
```
